768 devices in a mesh: section: 2 (over y_lo), lat: 4 (over x), lon: 96 (over z, y_hi, core).
Axes of the slice: x: 4, y: 8 (y_hi: 4, y_lo: 2; y = y_hi * 2 + y_lo), z: 12, core: 2. Of those that a mesh axis runs over, the one named last changes fastest.
Arguments:
- block_inputs: bfloat16 [2, 2, 24, 1152, 512], P('section', None, 'lat', 'lon'), may hold values from -6 to 6
- out_grads: bfloat16 [2, 2, 24, 1152, 512], P('section', None, 'lat', 'lon'), may hold values from -6 to 6
- offsets: int32 [2, 2], P('section'), may hold values from 1 to 11, as said below
- w_qkv: bfloat16 [2, 512, 1536], P('section'), may hold values from -0.25 to 0.25
- w_out: bfloat16 [2, 512, 512], P('section'), may hold values from -0.25 to 0.25
Outputs:
- d_input: bfloat16 [2, 2, 24, 1152, 512], P('section', None, 'lat', 'lon')
The draws below stay inside these ranges and needn't reach their ends.
Inputs may be any that keep to these rules, and one draw needn't show every extreme that they name: `offsets`: the first entry of each row is at least 1 and below 6, the second at least 1 and below 12.
All inputs are finite; a program needn't handle non-finite values.
Results may differ from the reference program's by a relative error of at most 0.0038.
Values may be sent and summed in bfloat16 or wider, within the bound.
No kernel may reach another device: no remote copies, remote signals or barrier semaphores. Data moves between devices by JAX's collectives and lax.ppermute only.
A program may use at most 32 MiB of HBM per device.

```python
import jax
import jax.numpy as jnp
from jax import lax

D = 512
HEADS = 16
LEVELS = 2
WLAT = 6
WLON = 12
NLAT = 24
NLON = 1152
N_SECTION = 2


def draw_offsets(key, part):
    lat_key, lon_key, pick_key = jax.random.split(key, 3)
    lat_part = jax.random.randint(lat_key, (N_SECTION,), 1, WLAT)
    lon_part = jax.random.randint(lon_key, (N_SECTION,), 1, WLON)
    chosen = jax.random.randint(pick_key, (), 0, N_SECTION)
    section_ids = jnp.arange(N_SECTION)
    lat_part = jnp.where(section_ids == chosen, 1, lat_part)
    lon_part = jnp.where(section_ids == chosen, WLON - 1, lon_part)
    return jnp.stack([lat_part, lon_part], axis=1).astype(jnp.int32)


def level_of(key, shape, pieces, least, largest):
    def one(axis_at, blocks):
        steps = jax.random.uniform(jax.random.fold_in(jax.random.fold_in(key, 6), axis_at), (blocks,), jnp.float32, least / len(pieces), largest / len(pieces))
        return jnp.repeat(jnp.exp(steps), shape[axis_at] // blocks).reshape((-1,) + (1,) * (len(shape) - axis_at - 1))

    factor_of = one(*pieces[0])
    for cut in pieces[1:]:
        factor_of = factor_of * one(*cut)
    return factor_of


def gaussian(stream_key, shape, spread, bound, cuts=(), held_as=jnp.bfloat16):
    drawn = jax.random.normal(stream_key, shape, jnp.float32) * spread
    if len(cuts) > 0:
        drawn = level_of(stream_key, shape, cuts, -0.22, 0.18) * drawn
    return jnp.clip(drawn, min=-bound, max=bound).astype(held_as)


def setup_inputs(seed: int = 0) -> dict:
    seeds = jax.random.split(jax.random.key(seed), 6)
    return {
        "block_inputs": gaussian(seeds[0], (N_SECTION, LEVELS, NLAT, NLON, D), 1.0, 6.0, ((0, 2), (2, 4), (3, 96))),
        "out_grads": gaussian(seeds[1], (N_SECTION, LEVELS, NLAT, NLON, D), 1.0, 6.0, ((0, 2), (2, 4), (3, 96))),
        "offsets": draw_offsets(jax.random.fold_in(seeds[5], 71), 0),
        "w_qkv": gaussian(seeds[3], (N_SECTION, D, 3 * D), D ** -0.5, 0.25, ((0, 2),)),
        "w_out": gaussian(seeds[4], (N_SECTION, D, D), D ** -0.5, 0.25, ((0, 2),)),
    }


EPSILON = 1e-05

def normalize(values):
    widened = values.astype(jnp.float32)
    centered = widened - lax.optimization_barrier(jnp.mean(widened, axis=-1, keepdims=True))
    inv_std = lax.rsqrt(lax.optimization_barrier(jnp.mean(centered * centered, axis=-1, keepdims=True)) + EPSILON)
    return (centered * inv_std, inv_std)

def to_windows(array_in):
    level_count, row_count, col_count, channels = array_in.shape
    shaped = array_in.reshape(level_count, row_count // WLAT, WLAT, col_count // WLON, WLON, channels)
    shaped = shaped.transpose(1, 3, 0, 2, 4, 5)
    return shaped.reshape(row_count // WLAT, col_count // WLON, level_count * WLAT * WLON, channels)

def from_windows(windowed, level_count, row_count, col_count):
    channels = windowed.shape[-1]
    shaped = windowed.reshape(row_count // WLAT, col_count // WLON, level_count, WLAT, WLON, channels)
    return shaped.transpose(2, 0, 3, 1, 4, 5).reshape(level_count, row_count, col_count, channels)

def window_grads(proj_win, grad_out, labels):
    win_count, tokens_win, triple = proj_win.shape
    feature_width = triple // 3
    head_size = feature_width // HEADS
    inv_root = 1.0 / head_size ** 0.5
    split_proj = proj_win.astype(jnp.float32).reshape(win_count, tokens_win, 3, HEADS, head_size)
    queries, keys_all, values_all = (split_proj[:, :, 0], split_proj[:, :, 1], split_proj[:, :, 2])
    grad_heads = grad_out.astype(jnp.float32).reshape(win_count, tokens_win, HEADS, head_size)
    scores = jnp.einsum('wphd,wrhd->whpr', queries, keys_all) * inv_root
    allowed = labels[:, None, :, None] == labels[:, None, None, :]
    weights_exp = jnp.where(allowed, jnp.exp(scores), 0.0)
    probability = weights_exp / lax.optimization_barrier(jnp.sum(weights_exp, axis=-1, keepdims=True))
    prob_bf16 = probability.astype(jnp.bfloat16).astype(jnp.float32)
    d_probability = jnp.einsum('wphd,wrhd->whpr', grad_heads, values_all)
    d_values = jnp.einsum('whpr,wphd->wrhd', prob_bf16, grad_heads)
    row_delta = lax.optimization_barrier(jnp.sum(probability * d_probability, axis=-1, keepdims=True))
    d_scores = (probability * (d_probability - row_delta)).astype(jnp.bfloat16).astype(jnp.float32)
    d_queries = jnp.einsum('whpr,wrhd->wphd', d_scores, keys_all) * inv_root
    d_keys = jnp.einsum('whpr,wphd->wrhd', d_scores, queries) * inv_root
    joined = jnp.stack([d_queries, d_keys, d_values], axis=2)
    return joined.reshape(win_count, tokens_win, triple).astype(jnp.bfloat16)

def section_grad(inputs, grad_in, labels, offset_row, w_qkv, w_out):
    level_count, lat_total, lon_total, feature_width = inputs.shape
    normed, inv_std = normalize(inputs)
    flat_normed = normed.astype(jnp.bfloat16).reshape(-1, feature_width)
    projected = jnp.dot(flat_normed, w_qkv, preferred_element_type=jnp.float32).astype(jnp.bfloat16)
    projected = projected.reshape(level_count, lat_total, lon_total, 3 * feature_width)
    grad_attn = jnp.dot(grad_in.reshape(-1, feature_width), w_out.T, preferred_element_type=jnp.float32)
    grad_attn = grad_attn.astype(jnp.bfloat16).reshape(level_count, lat_total, lon_total, feature_width)
    lat_shift = offset_row[0].astype(jnp.int32)
    lon_shift = offset_row[1].astype(jnp.int32)
    row_span = (lat_total // WLAT + 1) * WLAT

    def position(array_in):
        padding = [(0, 0), (WLAT, WLAT), (0, 0), (0, 0)]
        padded = jnp.pad(array_in, padding)
        region = lax.dynamic_slice_in_dim(padded, lat_shift, row_span, 1)
        return jnp.roll(region, -lon_shift, axis=2)
    proj_win = to_windows(position(projected))
    grad_win = to_windows(position(grad_attn))
    label_win = to_windows(position(labels[..., None]))[..., 0]

    def one_row(triple_in):
        return window_grads(triple_in[0], triple_in[1], triple_in[2])
    dproj_win = lax.map(one_row, (proj_win, grad_win, label_win))
    d_projected = from_windows(dproj_win, level_count, row_span, lon_total)
    d_projected = jnp.roll(d_projected, lon_shift, axis=2)
    d_projected = lax.dynamic_slice_in_dim(d_projected, (WLAT - lat_shift).astype(jnp.int32), lat_total, 1)
    d_normed = jnp.dot(d_projected.reshape(-1, 3 * feature_width), w_qkv.T, preferred_element_type=jnp.float32)
    d_normed = d_normed.reshape(level_count, lat_total, lon_total, feature_width)
    branch = inv_std * (d_normed - lax.optimization_barrier(jnp.mean(d_normed, axis=-1, keepdims=True)) - normed * lax.optimization_barrier(jnp.mean(d_normed * normed, axis=-1, keepdims=True)))
    return (grad_in.astype(jnp.float32) + branch).astype(jnp.bfloat16)

def reference(block_inputs, out_grads, offsets, w_qkv, w_out):
    labels = jnp.ones((block_inputs.shape[1], block_inputs.shape[2], block_inputs.shape[3]), jnp.int32)
    results = []
    for section_id in range(block_inputs.shape[0]):
        results.append(section_grad(block_inputs[section_id], out_grads[section_id], labels, offsets[section_id], w_qkv[section_id], w_out[section_id]))
    stacked = jnp.stack(results, axis=0)
    return jnp.roll(stacked, -1, axis=0)
```

```python
import jax
import jax.numpy as jnp
from jax import lax
from jax.experimental import pallas as pl
from jax.experimental.pallas import tpu as pltpu
from jax.sharding import PartitionSpec as P

HEADS = 16
WLAT = 6
WLON = 12
EPSILON = 1e-05
GROUP = 8


def shift(value, axes, moves):
    sizes = [lax.axis_size(axis) for axis in axes]
    pairs = [(0, 0)]
    for size, move in zip(sizes, moves):
        pairs = [
            (s * size + i, d * size + (i + move) % size) for s, d in pairs for i in range(size)
        ]
    return lax.ppermute(value, axes, pairs)


def dot(lhs, rhs, lhs_dim, rhs_dim):
    return lax.dot_general(
        lhs, rhs, (((lhs_dim,), (rhs_dim,)), ((), ())), preferred_element_type=jnp.float32
    )


def project_kernel(x_ref, w_ref, qkv_ref, normed_ref, inv_ref):
    widened = x_ref[...].astype(jnp.float32)
    centered = widened - jnp.mean(widened, axis=-1, keepdims=True)
    inv_std = lax.rsqrt(jnp.mean(centered * centered, axis=-1, keepdims=True) + EPSILON)
    normed = centered * inv_std
    normed_ref[...] = normed
    inv_ref[...] = inv_std
    qkv_ref[...] = dot(normed.astype(jnp.bfloat16), w_ref[...], 1, 0).astype(jnp.bfloat16)


def window_kernel(
    qkv_ref, normed_ref, inv_ref, grads_ref, w_qkv_ref, w_out_ref, key_ref, query_ref, out_ref,
    joined_ref,
):
    tokens, width = grads_ref.shape
    head = width // HEADS
    inv_root = 1.0 / head**0.5
    lanes = GROUP * head
    grads = grads_ref[...]
    grad_heads = dot(grads, w_out_ref[...], 1, 1).astype(jnp.bfloat16)
    allowed = key_ref[...] == query_ref[...]
    lane_head = lax.broadcasted_iota(jnp.int32, (tokens, lanes), 1) // head

    def stack(values):
        return jnp.concatenate(
            [jnp.where(lane_head == h, values, jnp.zeros_like(values)) for h in range(GROUP)],
            axis=0,
        )

    for group in range(HEADS // GROUP):
        low = group * lanes
        queries = qkv_ref[:, low : low + lanes]
        keys_all = qkv_ref[:, width + low : width + low + lanes]
        values_all = qkv_ref[:, 2 * width + low : 2 * width + low + lanes]
        query_stack = stack(queries)
        grad_stack = stack(grad_heads[:, low : low + lanes])
        scores = dot(keys_all, query_stack, 1, 1) * inv_root
        weights_exp = jnp.where(allowed, jnp.exp(scores), 0.0)
        probability = weights_exp * (1.0 / jnp.sum(weights_exp, axis=0, keepdims=True))
        d_probability = dot(values_all, grad_stack, 1, 1)
        delta = jnp.sum(probability * d_probability, axis=0, keepdims=True)
        d_scores = (probability * (d_probability - delta)).astype(jnp.bfloat16)
        d_values = dot(probability.astype(jnp.bfloat16), grad_stack, 1, 0)
        d_keys = dot(d_scores, query_stack, 1, 0) * inv_root
        spread = dot(d_scores, keys_all, 0, 0)
        d_queries = jnp.zeros((tokens, lanes), jnp.float32)
        for h in range(GROUP):
            d_queries = jnp.where(lane_head == h, spread[h * tokens : (h + 1) * tokens], d_queries)
        d_queries = d_queries * inv_root
        joined_ref[:, low : low + lanes] = d_queries.astype(jnp.bfloat16)
        joined_ref[:, width + low : width + low + lanes] = d_keys.astype(jnp.bfloat16)
        joined_ref[:, 2 * width + low : 2 * width + low + lanes] = d_values.astype(jnp.bfloat16)
    d_normed = dot(joined_ref[...], w_qkv_ref[...], 1, 1)
    normed = normed_ref[...]
    branch = inv_ref[...] * (
        d_normed
        - jnp.mean(d_normed, axis=-1, keepdims=True)
        - normed * jnp.mean(d_normed * normed, axis=-1, keepdims=True)
    )
    out_ref[...] = (grads.astype(jnp.float32) + branch).astype(jnp.bfloat16)


def local(block_inputs, out_grads, offsets, w_qkv, w_out):
    weights_in = w_qkv[0]
    weights_out = w_out[0]
    lat_shift = offsets[0, 0]
    lon_shift = offsets[0, 1]
    _, levels, rows, cols, width = block_inputs.shape
    tokens = levels * rows * cols
    vmem = pl.BlockSpec(memory_space=pltpu.VMEM)
    inputs = block_inputs[0].transpose(1, 2, 0, 3)
    grad_in = out_grads[0].transpose(1, 2, 0, 3)
    own_rows = jnp.arange(rows, dtype=jnp.int32)[:, None, None, None] < lat_shift
    own_cols = jnp.arange(cols, dtype=jnp.int32)[None, :, None, None] < lon_shift

    from_rows = shift(inputs, ("lat",), (1,))
    grads_rows = shift(grad_in, ("lat",), (1,))
    inputs = jnp.where(own_rows, inputs, from_rows)
    from_cols = shift(inputs, ("lon",), (1,))
    grad_in = jnp.where(own_rows, grad_in, grads_rows)
    grads_cols = shift(grad_in, ("lon",), (1,))
    inputs = jnp.where(own_cols, inputs, from_cols).reshape(tokens, width)
    qkv, normed, inv_std = pl.pallas_call(
        project_kernel,
        out_shape=(
            jax.ShapeDtypeStruct((tokens, 3 * width), jnp.bfloat16),
            jax.ShapeDtypeStruct((tokens, width), jnp.float32),
            jax.ShapeDtypeStruct((tokens, 1), jnp.float32),
        ),
        in_specs=[vmem, vmem],
        out_specs=(vmem, vmem, vmem),
        name="project",
    )(inputs, weights_in)

    row_of = jnp.arange(tokens, dtype=jnp.int32) // (levels * cols)
    label = ((row_of >= lat_shift) & (lax.axis_index("lat") == 0)).astype(jnp.float32)
    grad_in = jnp.where(own_cols, grad_in, grads_cols).reshape(tokens, width)
    result = pl.pallas_call(
        window_kernel,
        out_shape=jax.ShapeDtypeStruct((tokens, width), jnp.bfloat16),
        in_specs=[vmem] * 8,
        out_specs=vmem,
        scratch_shapes=[pltpu.VMEM((tokens, 3 * width), jnp.bfloat16)],
        name="window",
    )(
        qkv, normed, inv_std, grad_in, weights_in, weights_out,
        label[:, None], jnp.tile(label, GROUP)[None, :],
    )

    result = result.reshape(rows, cols, levels, width)
    back_cols = shift(result, ("lon",), (-1,))
    result = jnp.where(own_cols, result, back_cols)
    zero = jnp.zeros_like(result)
    kept = shift(jnp.where(own_rows, result, zero), ("section",), (-1,))
    moved = shift(jnp.where(own_rows, zero, result), ("section", "lat"), (-1, -1))
    return (kept + moved).transpose(2, 0, 1, 3)[None]


def solution(mesh):
    return jax.shard_map(
        local,
        mesh=mesh,
        in_specs=(
            P("section", None, "lat", "lon", None),
            P("section", None, "lat", "lon", None),
            P("section", None),
            P("section", None, None),
            P("section", None, None),
        ),
        out_specs=P("section", None, "lat", "lon", None),
        check_vma=False,
    )
```

```python
import jax
import jax.numpy as jnp
from jax import lax
from jax.experimental import pallas as pl
from jax.experimental.pallas import tpu as pltpu
from jax.sharding import PartitionSpec as P

HEADS = 16
WLAT = 6
WLON = 12
EPSILON = 1e-05
GROUP = 8


def shift(value, axis, move):
    count = lax.axis_size(axis)
    return lax.ppermute(value, axis, [(s, (s + move) % count) for s in range(count)])


def dot(lhs, rhs, lhs_dim, rhs_dim):
    return lax.dot_general(
        lhs, rhs, (((lhs_dim,), (rhs_dim,)), ((), ())), preferred_element_type=jnp.float32
    )


def exchange(arrays, dim, axis, cut, forward, home):
    size = arrays[0].shape[dim]
    low, high = (cut, size) if forward else (0, cut)
    parts = [lax.slice_in_dim(array, low, high, axis=dim) for array in arrays]
    strip = jnp.concatenate(parts, axis=0) if len(parts) > 1 else parts[0]
    strip = shift(strip, axis, 1 if forward != home else -1)
    out = []
    for k, array in enumerate(arrays):
        count = parts[k].shape[0]
        part = lax.slice_in_dim(strip, k * count, (k + 1) * count, axis=0)
        if forward:
            pieces = [lax.slice_in_dim(array, 0, cut, axis=dim), part]
        else:
            pieces = [part, lax.slice_in_dim(array, cut, size, axis=dim)]
        out.append(jnp.concatenate(pieces, axis=dim))
    return tuple(out)


def exchange_by(offset, size, arrays, dim, axis, home):
    branches = [
        lambda *values, cut=cut: exchange(values, dim, axis, cut, 2 * cut >= size, home)
        for cut in range(1, size)
    ]
    return lax.switch(offset - 1, branches, *arrays)


def window_kernel(
    scalars_ref, x_ref, grads_in_ref, w_qkv_ref, w_out_ref, out_ref, x_rows, grad_rows, joined_ref
):
    tokens, width = x_rows.shape
    head = width // HEADS
    inv_root = 1.0 / head**0.5
    lanes = GROUP * head
    levels = x_ref.shape[1]
    for i in range(tokens // levels):
        x_rows[levels * i : levels * (i + 1), :] = x_ref[i].astype(jnp.float32)
        grad_rows[levels * i : levels * (i + 1), :] = grads_in_ref[i].astype(jnp.float32)
    widened = x_rows[...]
    centered = widened - jnp.mean(widened, axis=-1, keepdims=True)
    inv_std = lax.rsqrt(jnp.mean(centered * centered, axis=-1, keepdims=True) + EPSILON)
    normed = centered * inv_std
    qkv = dot(normed.astype(jnp.bfloat16), w_qkv_ref[...], 1, 0).astype(jnp.bfloat16)
    grads = grad_rows[...]
    grad_heads = dot(grads.astype(jnp.bfloat16), w_out_ref[...], 1, 1).astype(jnp.bfloat16)

    cut = scalars_ref[0]
    key_at = lax.broadcasted_iota(jnp.int32, (tokens, 1), 0)
    lane = lax.broadcasted_iota(jnp.int32, (1, GROUP * tokens), 1)
    copy_of = jnp.zeros_like(lane)
    for h in range(1, GROUP):
        copy_of = jnp.where(lane >= h * tokens, h * tokens, copy_of)
    key_side = jnp.where(key_at >= cut, 1.0, 0.0)
    query_side = jnp.where(lane - copy_of >= cut, 1.0, 0.0)
    allowed = key_side == query_side
    lane_head = lax.broadcasted_iota(jnp.int32, (tokens, lanes), 1) // head

    def stack(values):
        return jnp.concatenate(
            [jnp.where(lane_head == h, values, jnp.zeros_like(values)) for h in range(GROUP)],
            axis=0,
        )

    for group in range(HEADS // GROUP):
        low = group * lanes
        queries = qkv[:, low : low + lanes]
        keys_all = qkv[:, width + low : width + low + lanes]
        values_all = qkv[:, 2 * width + low : 2 * width + low + lanes]
        query_stack = stack(queries)
        grad_stack = stack(grad_heads[:, low : low + lanes])
        scores = dot(keys_all, query_stack, 1, 1) * inv_root
        weights_exp = jnp.where(allowed, jnp.exp(scores), 0.0)
        probability = weights_exp * (1.0 / jnp.sum(weights_exp, axis=0, keepdims=True))
        d_probability = dot(values_all, grad_stack, 1, 1)
        delta = jnp.sum(probability * d_probability, axis=0, keepdims=True)
        d_scores = (probability * (d_probability - delta)).astype(jnp.bfloat16)
        d_values = dot(probability.astype(jnp.bfloat16), grad_stack, 1, 0)
        d_keys = dot(d_scores, query_stack, 1, 0) * inv_root
        spread = dot(d_scores, keys_all, 0, 0)
        d_queries = jnp.zeros((tokens, lanes), jnp.float32)
        for h in range(GROUP):
            d_queries = jnp.where(lane_head == h, spread[h * tokens : (h + 1) * tokens], d_queries)
        d_queries = d_queries * inv_root
        joined_ref[:, low : low + lanes] = d_queries.astype(jnp.bfloat16)
        joined_ref[:, width + low : width + low + lanes] = d_keys.astype(jnp.bfloat16)
        joined_ref[:, 2 * width + low : 2 * width + low + lanes] = d_values.astype(jnp.bfloat16)
    d_normed = dot(joined_ref[...], w_qkv_ref[...], 1, 1)
    branch = inv_std * (
        d_normed
        - jnp.mean(d_normed, axis=-1, keepdims=True)
        - normed * jnp.mean(d_normed * normed, axis=-1, keepdims=True)
    )
    x_rows[...] = grads + branch
    for i in range(tokens // levels):
        out_ref[i] = x_rows[levels * i : levels * (i + 1), :].astype(jnp.bfloat16)


def local(block_inputs, out_grads, offsets, w_qkv, w_out):
    lat_shift = offsets[0, 0]
    lon_shift = offsets[0, 1]
    _, levels, rows, cols, width = block_inputs.shape
    tokens = levels * rows * cols
    inputs = block_inputs[0].transpose(1, 2, 0, 3)
    grad_in = out_grads[0].transpose(1, 2, 0, 3)
    pair = (inputs, grad_in)
    pair = exchange_by(lat_shift, rows, pair, 0, "lat", False)
    pair = exchange_by(lon_shift, cols, pair, 1, "lon", False)

    lat_index = lax.axis_index("lat")
    edge = jnp.where(2 * lat_shift >= rows, 0, lax.axis_size("lat") - 1)
    cut = jnp.where(lat_index == edge, lat_shift * (levels * cols), tokens)
    vmem = pl.BlockSpec(memory_space=pltpu.VMEM)
    flat = (rows * cols, levels, width)
    result = pl.pallas_call(
        window_kernel,
        out_shape=pltpu.VMEM(flat, jnp.bfloat16),
        in_specs=[pl.BlockSpec(memory_space=pltpu.SMEM)] + [vmem] * 4,
        out_specs=vmem,
        scratch_shapes=[
            pltpu.VMEM((tokens, width), jnp.float32),
            pltpu.VMEM((tokens, width), jnp.float32),
            pltpu.VMEM((tokens, 3 * width), jnp.bfloat16),
        ],
        name="window",
    )(
        cut[None].astype(jnp.int32),
        *(
            pltpu.with_memory_space_constraint(value, pltpu.VMEM)
            for value in (pair[0].reshape(flat), pair[1].reshape(flat), w_qkv[0], w_out[0])
        ),
    )

    result = (result.reshape(rows, cols, levels, width),)
    result = exchange_by(lon_shift, cols, result, 1, "lon", True)
    result = exchange_by(lat_shift, rows, result, 0, "lat", True)
    return shift(result[0], "section", -1).transpose(2, 0, 1, 3)[None]


def solution(mesh):
    return jax.shard_map(
        local,
        mesh=mesh,
        in_specs=(
            P("section", None, "lat", "lon", None),
            P("section", None, "lat", "lon", None),
            P("section", None),
            P("section", None, None),
            P("section", None, None),
        ),
        out_specs=P("section", None, "lat", "lon", None),
        check_vma=False,
    )
```

```python
import functools

import jax
import jax.numpy as jnp
from jax import lax
from jax.experimental import pallas as pl
from jax.experimental.pallas import tpu as pltpu
from jax.sharding import PartitionSpec as P

HEADS = 16
WLAT = 6
WLON = 12
EPSILON = 1e-05
GROUP = 8


def shift(value, moves):
    axes = tuple(moves)
    pairs = [(0, 0)]
    for axis in axes:
        size, move = lax.axis_size(axis), moves[axis]
        pairs = [
            (s * size + i, d * size + (i + move) % size) for s, d in pairs for i in range(size)
        ]
    return lax.ppermute(value, axes, pairs)


def dot(lhs, rhs, lhs_dim, rhs_dim):
    return lax.dot_general(
        lhs, rhs, (((lhs_dim,), (rhs_dim,)), ((), ())), preferred_element_type=jnp.float32
    )


def directions(offsets_ref):
    lat_shift, lon_shift = offsets_ref[0, 0], offsets_ref[0, 1]
    return lat_shift, lon_shift, 2 * lat_shift >= WLAT, 2 * lon_shift >= WLON


def pack(offsets_ref, block, strips, cols_scratch):
    rows_ref, cols_ref, corner_ref = strips
    _, _, ahead_rows, ahead_cols = directions(offsets_ref)
    tokens = block.shape[0]
    half, line = tokens // 2, tokens // WLAT
    part = line // 2
    rows_ref[...] = jnp.where(ahead_rows, block[half:, :], block[:half, :]).astype(jnp.bfloat16)
    for r in range(WLAT):
        cols_scratch[r * part : (r + 1) * part, :] = jnp.where(
            ahead_cols,
            block[r * line + part : (r + 1) * line, :],
            block[r * line : r * line + part, :],
        )
    cols_ref[...] = cols_scratch[...].astype(jnp.bfloat16)
    corner_ref[...] = jnp.where(
        ahead_rows, cols_scratch[half // 2 :, :], cols_scratch[: half // 2, :]
    ).astype(jnp.bfloat16)


def unpack(offsets_ref, own_ref, strips, spread, cols_scratch):
    rows_ref, cols_ref, corner_ref = strips
    lat_shift, lon_shift, ahead_rows, ahead_cols = directions(offsets_ref)
    tokens = own_ref.shape[0]
    half, line = tokens // 2, tokens // WLAT
    part = line // 2
    level_count = line // WLON

    def given_rows(token_at, per_row):
        cut = lat_shift * per_row
        return jnp.where(ahead_rows, token_at - cut, cut - 1 - token_at) >= 0

    corner = corner_ref[...].astype(jnp.float32)
    cols_scratch[: half // 2, :] = corner
    cols_scratch[half // 2 :, :] = corner
    at_part = lax.broadcasted_iota(jnp.int32, (half, 1), 0)
    cols_scratch[...] = jnp.where(
        given_rows(at_part, part), cols_scratch[...], cols_ref[...].astype(jnp.float32)
    )
    for r in range(WLAT):
        piece = cols_scratch[r * part : (r + 1) * part, :]
        spread[r * line : r * line + part, :] = piece
        spread[r * line + part : (r + 1) * line, :] = piece
    at = lax.broadcasted_iota(jnp.int32, (tokens, 1), 0)
    row_start = jnp.zeros_like(at)
    for r in range(1, WLAT):
        row_start = jnp.where(at >= r * line, r * line, row_start)
    col_cut = lon_shift * level_count
    given_cols = jnp.where(ahead_cols, at - row_start - col_cut, col_cut - 1 - at + row_start) >= 0
    rows = rows_ref[...].astype(jnp.float32)
    straight = jnp.where(
        given_rows(at, line),
        jnp.concatenate([rows, rows], axis=0),
        own_ref[...].astype(jnp.float32),
    )
    return jnp.where(given_cols, spread[...], straight)


def pack_kernel(offsets_ref, x_ref, grads_ref, branch_ref, own_ref, rows_ref, cols_ref, corner_ref,
                block, cols_scratch):
    _, _, ahead_rows, ahead_cols = directions(offsets_ref)
    branch_ref[0] = 2 * ahead_rows.astype(jnp.int32) + ahead_cols.astype(jnp.int32)
    levels, width = x_ref.shape[1:]
    for i in range(x_ref.shape[0]):
        block[levels * i : levels * (i + 1), :width] = x_ref[i].astype(jnp.float32)
        block[levels * i : levels * (i + 1), width:] = grads_ref[i].astype(jnp.float32)
    own_ref[...] = block[...].astype(jnp.bfloat16)
    pack(offsets_ref, block, (rows_ref, cols_ref, corner_ref), cols_scratch)


def merge_kernel(offsets_ref, own_ref, rows_ref, cols_ref, corner_ref, out_ref, spread, cols_scratch):
    levels = out_ref.shape[1]
    strips = (rows_ref, cols_ref, corner_ref)
    spread[...] = unpack(offsets_ref, own_ref, strips, spread, cols_scratch)
    for i in range(out_ref.shape[0]):
        out_ref[i] = spread[levels * i : levels * (i + 1), :].astype(jnp.bfloat16)


def window_kernel(
    offsets_ref, lat_ref, own_ref, rows_ref, cols_ref, corner_ref, w_qkv_ref, w_out_ref,
    out_ref, rows_out_ref, cols_out_ref, corner_out_ref,
    spread, cols_scratch, result, result_cols, joined_ref, *, lat_count,
):
    tokens, width = result.shape
    head = width // HEADS
    inv_root = 1.0 / head**0.5
    lanes = GROUP * head
    both = unpack(offsets_ref, own_ref, (rows_ref, cols_ref, corner_ref), spread, cols_scratch)
    widened, grads = both[:, :width], both[:, width:]
    centered = widened - jnp.mean(widened, axis=-1, keepdims=True)
    inv_std = lax.rsqrt(jnp.mean(centered * centered, axis=-1, keepdims=True) + EPSILON)
    normed = centered * inv_std
    qkv = dot(normed.astype(jnp.bfloat16), w_qkv_ref[...], 1, 0).astype(jnp.bfloat16)
    grad_heads = dot(grads.astype(jnp.bfloat16), w_out_ref[...], 1, 1).astype(jnp.bfloat16)

    lat_shift, _, ahead_rows, _ = directions(offsets_ref)
    edge = jnp.where(ahead_rows, 0, lat_count - 1)
    cut = jnp.where(lat_ref[0] == edge, lat_shift * (tokens // WLAT), tokens)
    key_at = lax.broadcasted_iota(jnp.int32, (tokens, 1), 0)
    lane = lax.broadcasted_iota(jnp.int32, (1, GROUP * tokens), 1)
    copy_of = jnp.zeros_like(lane)
    for h in range(1, GROUP):
        copy_of = jnp.where(lane >= h * tokens, h * tokens, copy_of)
    key_side = jnp.where(key_at >= cut, 1.0, 0.0)
    query_side = jnp.where(lane - copy_of >= cut, 1.0, 0.0)
    allowed = key_side == query_side
    lane_head = lax.broadcasted_iota(jnp.int32, (tokens, lanes), 1) // head

    def stack(values):
        return jnp.concatenate(
            [jnp.where(lane_head == h, values, jnp.zeros_like(values)) for h in range(GROUP)],
            axis=0,
        )

    for group in range(HEADS // GROUP):
        low = group * lanes
        queries = qkv[:, low : low + lanes]
        keys_all = qkv[:, width + low : width + low + lanes]
        values_all = qkv[:, 2 * width + low : 2 * width + low + lanes]
        query_stack = stack(queries)
        grad_stack = stack(grad_heads[:, low : low + lanes])
        scores = dot(keys_all, query_stack, 1, 1) * inv_root
        weights_exp = jnp.where(allowed, jnp.exp(scores), 0.0)
        probability = weights_exp * (1.0 / jnp.sum(weights_exp, axis=0, keepdims=True))
        d_probability = dot(values_all, grad_stack, 1, 1)
        delta = jnp.sum(probability * d_probability, axis=0, keepdims=True)
        d_scores = (probability * (d_probability - delta)).astype(jnp.bfloat16)
        d_values = dot(probability.astype(jnp.bfloat16), grad_stack, 1, 0)
        d_keys = dot(d_scores, query_stack, 1, 0) * inv_root
        by_query = dot(d_scores, keys_all, 0, 0)
        d_queries = jnp.zeros((tokens, lanes), jnp.float32)
        for h in range(GROUP):
            d_queries = jnp.where(
                lane_head == h, by_query[h * tokens : (h + 1) * tokens], d_queries
            )
        d_queries = d_queries * inv_root
        joined_ref[:, low : low + lanes] = d_queries.astype(jnp.bfloat16)
        joined_ref[:, width + low : width + low + lanes] = d_keys.astype(jnp.bfloat16)
        joined_ref[:, 2 * width + low : 2 * width + low + lanes] = d_values.astype(jnp.bfloat16)
    d_normed = dot(joined_ref[...], w_qkv_ref[...], 1, 1)
    branch = inv_std * (
        d_normed
        - jnp.mean(d_normed, axis=-1, keepdims=True)
        - normed * jnp.mean(d_normed * normed, axis=-1, keepdims=True)
    )
    result[...] = grads + branch
    out_ref[...] = result[...].astype(jnp.bfloat16)
    pack(offsets_ref, result, (rows_out_ref, cols_out_ref, corner_out_ref), result_cols)


def send(branch, strips, sign):
    def moved(ahead_rows, ahead_cols):
        lat = sign if ahead_rows else -sign
        lon = sign if ahead_cols else -sign

        def run(rows, cols, corner):
            return (
                shift(rows, {"lat": lat}),
                shift(cols, {"lon": lon}),
                shift(corner, {"lat": lat, "lon": lon}),
            )

        return run

    return lax.switch(branch, [moved(a, b) for a in (False, True) for b in (False, True)], *strips)


def local(block_inputs, out_grads, offsets, w_qkv, w_out):
    _, levels, rows, cols, width = block_inputs.shape
    tokens = levels * rows * cols
    flat = (rows * cols, levels, width)
    vmem = pl.BlockSpec(memory_space=pltpu.VMEM)
    smem = pl.BlockSpec(memory_space=pltpu.SMEM)

    def strip_shapes(channels):
        return tuple(
            pltpu.VMEM((count, channels), jnp.bfloat16)
            for count in (tokens // 2, tokens // 2, tokens // 4)
        )

    def block_scratch(channels):
        return [
            pltpu.VMEM((tokens, channels), jnp.float32),
            pltpu.VMEM((tokens // 2, channels), jnp.float32),
        ]

    def held(values):
        return [pltpu.with_memory_space_constraint(value, pltpu.VMEM) for value in values]

    branch, own, *strips = pl.pallas_call(
        pack_kernel,
        out_shape=(
            jax.ShapeDtypeStruct((1,), jnp.int32),
            pltpu.VMEM((tokens, 2 * width), jnp.bfloat16),
            *strip_shapes(2 * width),
        ),
        in_specs=[smem, vmem, vmem],
        out_specs=(smem, vmem, vmem, vmem, vmem),
        scratch_shapes=block_scratch(2 * width),
        name="pack",
    )(
        offsets,
        block_inputs[0].transpose(1, 2, 0, 3).reshape(flat),
        out_grads[0].transpose(1, 2, 0, 3).reshape(flat),
    )
    strips = send(branch[0], strips, 1)
    result, *strips = pl.pallas_call(
        functools.partial(window_kernel, lat_count=lax.axis_size("lat")),
        out_shape=(pltpu.VMEM((tokens, width), jnp.bfloat16), *strip_shapes(width)),
        in_specs=[smem, smem] + [vmem] * 6,
        out_specs=(vmem,) * 4,
        scratch_shapes=[
            *block_scratch(2 * width),
            *block_scratch(width),
            pltpu.VMEM((tokens, 3 * width), jnp.bfloat16),
        ],
        name="window",
    )(offsets, lax.axis_index("lat").reshape(1), *held((own, *strips, w_qkv[0], w_out[0])))
    strips = send(branch[0], strips, -1)
    merged = pl.pallas_call(
        merge_kernel,
        out_shape=pltpu.VMEM(flat, jnp.bfloat16),
        in_specs=[smem] + [vmem] * 4,
        out_specs=vmem,
        scratch_shapes=block_scratch(width),
        name="merge",
    )(offsets, *held((result, *strips)))
    merged = merged.reshape(rows, cols, levels, width).transpose(2, 0, 1, 3)[None]
    return shift(merged, {"section": -1})


def solution(mesh):
    return jax.shard_map(
        local,
        mesh=mesh,
        in_specs=(
            P("section", None, "lat", "lon", None),
            P("section", None, "lat", "lon", None),
            P("section", None),
            P("section", None, None),
            P("section", None, None),
        ),
        out_specs=P("section", None, "lat", "lon", None),
        check_vma=False,
    )
```

```python
import functools

import jax
import jax.numpy as jnp
from jax import lax
from jax.experimental import pallas as pl
from jax.experimental.pallas import tpu as pltpu
from jax.sharding import PartitionSpec as P

HEADS = 16
WLAT = 6
WLON = 12
EPSILON = 1e-05
GROUP = 8


def shift(value, axis, move):
    count = lax.axis_size(axis)
    return lax.ppermute(value, axis, [(s, (s + move) % count) for s in range(count)])


def dot(lhs, rhs, lhs_dim, rhs_dim):
    return lax.dot_general(
        lhs, rhs, (((lhs_dim,), (rhs_dim,)), ((), ())), preferred_element_type=jnp.float32
    )


def exchange(array, dim, axis, cut, size, home):
    forward = 2 * cut >= size
    total = array.shape[dim]
    at = cut * (total // size)
    low, high = (at, total) if forward else (0, at)
    strip = shift(
        lax.slice_in_dim(array, low, high, axis=dim), axis, 1 if forward != home else -1
    )
    if forward:
        pieces = [lax.slice_in_dim(array, 0, at, axis=dim), strip]
    else:
        pieces = [strip, lax.slice_in_dim(array, at, total, axis=dim)]
    return jnp.concatenate(pieces, axis=dim)


def exchange_by(branch, size, array, dim, axis, home):
    branches = [
        lambda value, cut=cut: exchange(value, dim, axis, cut, size, home)
        for cut in range(1, size)
    ]
    return lax.switch(branch, branches, array)


def pack_kernel(offsets_ref, x_ref, grads_ref, lat_branch_ref, lon_branch_ref, out_ref, block):
    lat_branch_ref[0] = offsets_ref[0, 0] - 1
    lon_branch_ref[0] = offsets_ref[0, 1] - 1
    levels, width = x_ref.shape[1:]
    for i in range(x_ref.shape[0]):
        block[levels * i : levels * (i + 1), :width] = x_ref[i].astype(jnp.float32)
        block[levels * i : levels * (i + 1), width:] = grads_ref[i].astype(jnp.float32)
    out_ref[...] = block[...].astype(jnp.bfloat16)


def reorder_kernel(in_ref, out_ref, before, after):
    levels = before.shape[0] // (WLAT * WLON)
    before[...] = in_ref[...].astype(jnp.float32)
    for r in range(WLAT):
        for c in range(WLON):
            low, to = levels * (r * WLON + c), levels * (c * WLAT + r)
            after[to : to + levels, :] = before[low : low + levels, :]
    out_ref[...] = after[...].astype(jnp.bfloat16)


def window_kernel(
    offsets_ref, lat_ref, both_ref, w_out_ref, w_qkv_hbm,
    out_ref, result, joined_ref, w_qkv_ref, sem, *, lat_count,
):
    fetch = pltpu.make_async_copy(w_qkv_hbm, w_qkv_ref, sem)
    fetch.start()
    tokens, width = result.shape
    head = width // HEADS
    inv_root = 1.0 / head**0.5
    lanes = GROUP * head
    levels = out_ref.shape[1]
    widened = both_ref[:, :width].astype(jnp.float32)
    centered = widened - jnp.mean(widened, axis=-1, keepdims=True)
    inv_std = lax.rsqrt(jnp.mean(centered * centered, axis=-1, keepdims=True) + EPSILON)
    normed = centered * inv_std
    grads = both_ref[:, width:]
    grad_heads = dot(grads, w_out_ref[...], 1, 1).astype(jnp.bfloat16)
    fetch.wait()
    qkv = dot(normed.astype(jnp.bfloat16), w_qkv_ref[...], 1, 0).astype(jnp.bfloat16)

    lat_shift = offsets_ref[0, 0]
    edge = jnp.where(2 * lat_shift >= WLAT, 0, lat_count - 1)
    line = WLAT * levels
    cut = jnp.where(lat_ref[0] == edge, lat_shift * levels, line)

    def place_in_column(at, count):
        start = jnp.zeros_like(at)
        for c in range(1, count // line):
            start = jnp.where(at >= c * line, c * line, start)
        return at - start

    key_at = place_in_column(lax.broadcasted_iota(jnp.int32, (tokens, 1), 0), tokens)
    lane = lax.broadcasted_iota(jnp.int32, (1, GROUP * tokens), 1)
    query_at = place_in_column(lane, GROUP * tokens)
    key_side = jnp.where(key_at >= cut, 1.0, 0.0)
    query_side = jnp.where(query_at >= cut, 1.0, 0.0)
    allowed = key_side == query_side
    lane_head = lax.broadcasted_iota(jnp.int32, (tokens, lanes), 1) // head

    def stack(values):
        return jnp.concatenate(
            [jnp.where(lane_head == h, values, jnp.zeros_like(values)) for h in range(GROUP)],
            axis=0,
        )

    for group in range(HEADS // GROUP):
        low = group * lanes
        queries = qkv[:, low : low + lanes]
        keys_all = qkv[:, width + low : width + low + lanes]
        values_all = qkv[:, 2 * width + low : 2 * width + low + lanes]
        query_stack = stack(queries)
        grad_stack = stack(grad_heads[:, low : low + lanes])
        scores = dot(keys_all, query_stack, 1, 1) * inv_root
        weights_exp = jnp.where(allowed, jnp.exp(scores), 0.0)
        probability = weights_exp * (1.0 / jnp.sum(weights_exp, axis=0, keepdims=True))
        d_probability = dot(values_all, grad_stack, 1, 1)
        delta = jnp.sum(probability * d_probability, axis=0, keepdims=True)
        d_scores = (probability * (d_probability - delta)).astype(jnp.bfloat16)
        d_values = dot(probability.astype(jnp.bfloat16), grad_stack, 1, 0)
        d_keys = dot(d_scores, query_stack, 1, 0) * inv_root
        spread = dot(d_scores, keys_all, 0, 0)
        d_queries = jnp.zeros((tokens, lanes), jnp.float32)
        for h in range(GROUP):
            d_queries = jnp.where(lane_head == h, spread[h * tokens : (h + 1) * tokens], d_queries)
        d_queries = d_queries * inv_root
        joined_ref[:, low : low + lanes] = d_queries.astype(jnp.bfloat16)
        joined_ref[:, width + low : width + low + lanes] = d_keys.astype(jnp.bfloat16)
        joined_ref[:, 2 * width + low : 2 * width + low + lanes] = d_values.astype(jnp.bfloat16)
    d_normed = dot(joined_ref[...], w_qkv_ref[...], 1, 1)
    branch = inv_std * (
        d_normed
        - jnp.mean(d_normed, axis=-1, keepdims=True)
        - normed * jnp.mean(d_normed * normed, axis=-1, keepdims=True)
    )
    result[...] = grads.astype(jnp.float32) + branch
    for r in range(WLAT):
        for c in range(WLON):
            low = levels * (c * WLAT + r)
            out_ref[r * WLON + c] = result[low : low + levels, :].astype(jnp.bfloat16)


def local(block_inputs, out_grads, offsets, w_qkv, w_out):
    _, levels, rows, cols, width = block_inputs.shape
    tokens = levels * rows * cols
    flat = (rows * cols, levels, width)
    vmem = pl.BlockSpec(memory_space=pltpu.VMEM)
    smem = pl.BlockSpec(memory_space=pltpu.SMEM)
    both = (tokens, 2 * width)

    def held(*values):
        return [pltpu.with_memory_space_constraint(value, pltpu.VMEM) for value in values]

    lat_branch, lon_branch, block = pl.pallas_call(
        pack_kernel,
        out_shape=(
            jax.ShapeDtypeStruct((1,), jnp.int32),
            jax.ShapeDtypeStruct((1,), jnp.int32),
            pltpu.VMEM(both, jnp.bfloat16),
        ),
        in_specs=[smem, vmem, vmem],
        out_specs=(smem, smem, vmem),
        scratch_shapes=[pltpu.VMEM(both, jnp.float32)],
        name="pack",
    )(
        offsets,
        block_inputs[0].transpose(1, 2, 0, 3).reshape(flat),
        out_grads[0].transpose(1, 2, 0, 3).reshape(flat),
    )
    lat_branch, lon_branch = lat_branch[0], lon_branch[0]
    block = exchange_by(lat_branch, rows, block, 0, "lat", False)
    block = pl.pallas_call(
        reorder_kernel,
        out_shape=pltpu.VMEM(both, jnp.bfloat16),
        in_specs=[vmem],
        out_specs=vmem,
        scratch_shapes=[pltpu.VMEM(both, jnp.float32)] * 2,
        name="reorder",
    )(*held(block))
    block = exchange_by(lon_branch, cols, block, 0, "lon", False)
    result = pl.pallas_call(
        functools.partial(window_kernel, lat_count=lax.axis_size("lat")),
        out_shape=pltpu.VMEM(flat, jnp.bfloat16),
        in_specs=[smem, smem, vmem, vmem, pl.BlockSpec(memory_space=pl.ANY)],
        out_specs=vmem,
        scratch_shapes=[
            pltpu.VMEM((tokens, width), jnp.float32),
            pltpu.VMEM((tokens, 3 * width), jnp.bfloat16),
            pltpu.VMEM(w_qkv.shape[1:], jnp.bfloat16),
            pltpu.SemaphoreType.DMA,
        ],
        name="window",
    )(
        offsets,
        lax.axis_index("lat").reshape(1),
        *held(block, w_out[0]),
        pltpu.with_memory_space_constraint(w_qkv[0], pltpu.HBM),
    )

    result = result.reshape(rows, cols, levels, width)
    result = exchange_by(lon_branch, cols, result, 1, "lon", True)
    result = exchange_by(lat_branch, rows, result, 0, "lat", True)
    return shift(result.transpose(2, 0, 1, 3)[None], "section", -1)


def solution(mesh):
    return jax.shard_map(
        local,
        mesh=mesh,
        in_specs=(
            P("section", None, "lat", "lon", None),
            P("section", None, "lat", "lon", None),
            P("section", None),
            P("section", None, None),
            P("section", None, None),
        ),
        out_specs=P("section", None, "lat", "lon", None),
        check_vma=False,
    )
```

```python
import functools

import jax
import jax.numpy as jnp
from jax import lax
from jax.experimental import pallas as pl
from jax.experimental.pallas import tpu as pltpu
from jax.sharding import PartitionSpec as P

HEADS = 16
WLAT = 6
WLON = 12
EPSILON = 1e-05
GROUP = 8


def shift(value, axis, move):
    count = lax.axis_size(axis)
    return lax.ppermute(value, axis, [(s, (s + move) % count) for s in range(count)])


def dot(lhs, rhs, lhs_dim, rhs_dim):
    return lax.dot_general(
        lhs, rhs, (((lhs_dim,), (rhs_dim,)), ((), ())), preferred_element_type=jnp.float32
    )


def exchange(array, dim, axis, cut, size, home):
    forward = 2 * cut >= size
    total = array.shape[dim]
    at = cut * (total // size)
    low, high = (at, total) if forward else (0, at)
    strip = shift(
        lax.slice_in_dim(array, low, high, axis=dim), axis, 1 if forward != home else -1
    )
    if forward:
        pieces = [lax.slice_in_dim(array, 0, at, axis=dim), strip]
    else:
        pieces = [strip, lax.slice_in_dim(array, at, total, axis=dim)]
    return jnp.concatenate(pieces, axis=dim)


def exchange_by(branch, size, array, dim, axis, home, weights=()):
    def run(cut):
        def move(value, *weights):
            moved = exchange(value, dim, axis, cut, size, home)
            return moved, *(fetch(*weights) if weights else ())

        return move

    return lax.switch(branch, [run(cut) for cut in range(1, size)], array, *weights)


def fetch(w_qkv, w_out):
    return pl.pallas_call(
        fetch_kernel,
        out_shape=(pltpu.VMEM(w_out.shape, w_out.dtype),) * 4,
        in_specs=[pl.BlockSpec(memory_space=pl.ANY)] * 2,
        out_specs=(pl.BlockSpec(memory_space=pltpu.VMEM),) * 4,
        scratch_shapes=[pltpu.SemaphoreType.DMA((4,))],
        name="fetch",
    )(*(pltpu.with_memory_space_constraint(w, pltpu.HBM) for w in (w_qkv, w_out)))


def pack_kernel(
    offsets_hbm, x_hbm, grads_hbm, branch_ref, shift_ref, out_ref,
    offsets_ref, x_ref, grads_ref, block, sems,
):
    copies = [
        pltpu.make_async_copy(source, target, sems.at[k])
        for k, (source, target) in enumerate(
            ((offsets_hbm, offsets_ref), (x_hbm, x_ref), (grads_hbm, grads_ref))
        )
    ]
    for copy in copies:
        copy.start()
    levels, width = x_ref.shape[1:]
    copies[0].wait()
    branch_ref[0] = (offsets_ref[0, 0] - 1) * 16 + offsets_ref[0, 1] - 1
    shift_ref[...] = jnp.full(shift_ref.shape, offsets_ref[0, 0], jnp.int32)
    for copy, ref, low in ((copies[1], x_ref, 0), (copies[2], grads_ref, width)):
        copy.wait()
        for i in range(ref.shape[0]):
            block[levels * i : levels * (i + 1), low : low + width] = ref[i].astype(jnp.float32)
    out_ref[...] = block[...].astype(jnp.bfloat16)


def fetch_kernel(w_qkv_hbm, w_out_hbm, *refs):
    *targets, sems = refs
    width = w_out_hbm.shape[1]
    copies = []
    for k, target in enumerate(targets):
        source = w_qkv_hbm.at[:, k * width : (k + 1) * width] if k < 3 else w_out_hbm
        copies.append(pltpu.make_async_copy(source, target, sems.at[k]))
    for copy in copies:
        copy.start()
    for copy in copies:
        copy.wait()


def reorder_kernel(in_ref, out_ref, before, after):
    levels = before.shape[0] // (WLAT * WLON)
    before[...] = in_ref[...].astype(jnp.float32)
    for r in range(WLAT):
        for c in range(WLON):
            low, to = levels * (r * WLON + c), levels * (c * WLAT + r)
            after[to : to + levels, :] = before[low : low + levels, :]
    out_ref[...] = after[...].astype(jnp.bfloat16)


def window_kernel(
    shift_ref, both_ref, w_query_ref, w_key_ref, w_value_ref, w_out_ref,
    out_ref, result, joined_ref, *, lat_count,
):
    tokens, width = result.shape
    head = width // HEADS
    inv_root = 1.0 / head**0.5
    lanes = GROUP * head
    levels = out_ref.shape[1]
    widened = both_ref[:, :width].astype(jnp.float32)
    centered = widened - jnp.mean(widened, axis=-1, keepdims=True)
    inv_std = lax.rsqrt(jnp.mean(centered * centered, axis=-1, keepdims=True) + EPSILON)
    normed = centered * inv_std
    grads = both_ref[:, width:]
    grad_heads = dot(grads, w_out_ref[...], 1, 1).astype(jnp.bfloat16)
    weights = (w_query_ref, w_key_ref, w_value_ref)
    normed_bf16 = normed.astype(jnp.bfloat16)
    qkv = [dot(normed_bf16, w_ref[...], 1, 0).astype(jnp.bfloat16) for w_ref in weights]

    lat_shift = shift_ref[:1, :1]
    edge = jnp.where(2 * lat_shift >= WLAT, 0, lat_count - 1)
    line = WLAT * levels
    cut = jnp.where(lax.axis_index("lat") == edge, lat_shift * levels, line)

    def place_in_column(at, count):
        start = jnp.zeros_like(at)
        for c in range(1, count // line):
            start = jnp.where(at >= c * line, c * line, start)
        return at - start

    key_at = place_in_column(lax.broadcasted_iota(jnp.int32, (tokens, 1), 0), tokens)
    lane = lax.broadcasted_iota(jnp.int32, (1, GROUP * tokens), 1)
    query_at = place_in_column(lane, GROUP * tokens)
    key_side = jnp.where(key_at >= cut, 1.0, 0.0)
    query_side = jnp.where(query_at >= cut, 1.0, 0.0)
    allowed = key_side == query_side
    lane_head = lax.broadcasted_iota(jnp.int32, (tokens, lanes), 1) // head

    def stack(values):
        return jnp.concatenate(
            [jnp.where(lane_head == h, values, jnp.zeros_like(values)) for h in range(GROUP)],
            axis=0,
        )

    for group in range(HEADS // GROUP):
        low = group * lanes
        queries, keys_all, values_all = (part[:, low : low + lanes] for part in qkv)
        query_stack = stack(queries)
        grad_stack = stack(grad_heads[:, low : low + lanes])
        scores = dot(keys_all, query_stack, 1, 1) * inv_root
        weights_exp = jnp.where(allowed, jnp.exp(scores), 0.0)
        probability = weights_exp * (1.0 / jnp.sum(weights_exp, axis=0, keepdims=True))
        d_probability = dot(values_all, grad_stack, 1, 1)
        delta = jnp.sum(probability * d_probability, axis=0, keepdims=True)
        d_scores = (probability * (d_probability - delta)).astype(jnp.bfloat16)
        d_values = dot(probability.astype(jnp.bfloat16), grad_stack, 1, 0)
        d_keys = dot(d_scores, query_stack, 1, 0) * inv_root
        spread = dot(d_scores, keys_all, 0, 0)
        d_queries = jnp.zeros((tokens, lanes), jnp.float32)
        for h in range(GROUP):
            d_queries = jnp.where(lane_head == h, spread[h * tokens : (h + 1) * tokens], d_queries)
        d_queries = d_queries * inv_root
        joined_ref[:, low : low + lanes] = d_queries.astype(jnp.bfloat16)
        joined_ref[:, width + low : width + low + lanes] = d_keys.astype(jnp.bfloat16)
        joined_ref[:, 2 * width + low : 2 * width + low + lanes] = d_values.astype(jnp.bfloat16)
    d_normed = sum(
        dot(joined_ref[:, k * width : (k + 1) * width], w_ref[...], 1, 1)
        for k, w_ref in enumerate(weights)
    )
    branch = inv_std * (
        d_normed
        - jnp.mean(d_normed, axis=-1, keepdims=True)
        - normed * jnp.mean(d_normed * normed, axis=-1, keepdims=True)
    )
    result[...] = grads.astype(jnp.float32) + branch
    for r in range(WLAT):
        for c in range(WLON):
            low = levels * (c * WLAT + r)
            out_ref[r * WLON + c] = result[low : low + levels, :].astype(jnp.bfloat16)


def local(block_inputs, out_grads, offsets, w_qkv, w_out):
    _, levels, rows, cols, width = block_inputs.shape
    tokens = levels * rows * cols
    flat = (rows * cols, levels, width)
    vmem = pl.BlockSpec(memory_space=pltpu.VMEM)
    smem = pl.BlockSpec(memory_space=pltpu.SMEM)
    both = (tokens, 2 * width)

    def held(*values):
        return [pltpu.with_memory_space_constraint(value, pltpu.VMEM) for value in values]

    hbm = pl.BlockSpec(memory_space=pl.ANY)
    branch, lat_shift, block = pl.pallas_call(
        pack_kernel,
        out_shape=(
            jax.ShapeDtypeStruct((1,), jnp.int32),
            pltpu.VMEM((8, 128), jnp.int32),
            pltpu.VMEM(both, jnp.bfloat16),
        ),
        in_specs=[hbm] * 3,
        out_specs=(smem, vmem, vmem),
        scratch_shapes=[
            pltpu.SMEM(offsets.shape, jnp.int32),
            pltpu.VMEM(flat, jnp.bfloat16),
            pltpu.VMEM(flat, jnp.bfloat16),
            pltpu.VMEM(both, jnp.float32),
            pltpu.SemaphoreType.DMA((3,)),
        ],
        name="pack",
    )(
        offsets,
        block_inputs[0].transpose(1, 2, 0, 3).reshape(flat),
        out_grads[0].transpose(1, 2, 0, 3).reshape(flat),
    )
    lat_branch, lon_branch = branch[0] >> 4, branch[0] & 15
    (block,) = exchange_by(lat_branch, rows, block, 0, "lat", False)
    block = pl.pallas_call(
        reorder_kernel,
        out_shape=pltpu.VMEM(both, jnp.bfloat16),
        in_specs=[vmem],
        out_specs=vmem,
        scratch_shapes=[pltpu.VMEM(both, jnp.float32)] * 2,
        name="reorder",
    )(*held(block))
    block, *weights = exchange_by(
        lon_branch, cols, block, 0, "lon", False, (w_qkv[0], w_out[0])
    )
    result = pl.pallas_call(
        functools.partial(window_kernel, lat_count=lax.axis_size("lat")),
        out_shape=pltpu.VMEM(flat, jnp.bfloat16),
        in_specs=[vmem] * 6,
        out_specs=vmem,
        scratch_shapes=[
            pltpu.VMEM((tokens, width), jnp.float32),
            pltpu.VMEM((tokens, 3 * width), jnp.bfloat16),
        ],
        name="window",
    )(*held(lat_shift, block, *weights))

    result = result.reshape(rows, cols, levels, width)
    (result,) = exchange_by(lon_branch, cols, result, 1, "lon", True)
    (result,) = exchange_by(lat_branch, rows, result, 0, "lat", True)
    return shift(result.transpose(2, 0, 1, 3)[None], "section", -1)


def solution(mesh):
    return jax.shard_map(
        local,
        mesh=mesh,
        in_specs=(
            P("section", None, "lat", "lon", None),
            P("section", None, "lat", "lon", None),
            P("section", None),
            P("section", None, None),
            P("section", None, None),
        ),
        out_specs=P("section", None, "lat", "lon", None),
        check_vma=False,
    )
```

```python
import functools

import jax
import jax.numpy as jnp
from jax import lax
from jax.experimental import pallas as pl
from jax.experimental.pallas import tpu as pltpu
from jax.sharding import PartitionSpec as P

HEADS = 16
WLAT = 6
WLON = 12
EPSILON = 1e-05
GROUP = 8


def shift(value, **moves):
    axes = tuple(moves)
    pairs = [(0, 0)]
    for axis in axes:
        size, move = lax.axis_size(axis), moves[axis]
        pairs = [
            (s * size + i, d * size + (i + move) % size) for s, d in pairs for i in range(size)
        ]
    return lax.ppermute(value, axes, pairs)


def dot(lhs, rhs, lhs_dim, rhs_dim):
    return lax.dot_general(
        lhs, rhs, (((lhs_dim,), (rhs_dim,)), ((), ())), preferred_element_type=jnp.float32
    )


def exchange(array, axis, cut, size, home):
    forward = 2 * cut >= size
    total = array.shape[0]
    at = cut * (total // size)
    low, high = (at, total) if forward else (0, at)
    strip = shift(array[low:high], **{axis: 1 if forward != home else -1})
    pieces = [array[:at], strip] if forward else [strip, array[at:]]
    return jnp.concatenate(pieces, axis=0)


def exchange_by(branch, size, array, axis, home, weights=()):
    def run(cut):
        def move(value, *weights):
            moved = exchange(value, axis, cut, size, home)
            return moved, *(fetch(*weights) if weights else ())

        return move

    return lax.switch(branch, [run(cut) for cut in range(1, size)], array, *weights)


def fetch(w_qkv, w_out):
    return pl.pallas_call(
        fetch_kernel,
        out_shape=(pltpu.VMEM(w_out.shape, w_out.dtype),) * 4,
        in_specs=[pl.BlockSpec(memory_space=pl.ANY)] * 2,
        out_specs=(pl.BlockSpec(memory_space=pltpu.VMEM),) * 4,
        scratch_shapes=[pltpu.SemaphoreType.DMA((4,))],
        name="fetch",
    )(*(pltpu.with_memory_space_constraint(w, pltpu.HBM) for w in (w_qkv, w_out)))


def pack_kernel(
    offsets_hbm, x_hbm, grads_hbm, lat_branch_ref, lon_branch_ref, shift_ref, out_ref,
    offsets_ref, x_ref, grads_ref, block, sems,
):
    copies = [
        pltpu.make_async_copy(source, target, sems.at[k])
        for k, (source, target) in enumerate(
            ((offsets_hbm, offsets_ref), (x_hbm, x_ref), (grads_hbm, grads_ref))
        )
    ]
    for copy in copies:
        copy.start()
    levels, width = x_ref.shape[1:]
    copies[0].wait()
    lat_branch_ref[0] = offsets_ref[0, 0] - 1
    lon_branch_ref[0] = offsets_ref[0, 1] - 1
    shift_ref[...] = jnp.full(shift_ref.shape, offsets_ref[0, 0], jnp.int32)
    for copy, ref, low in ((copies[1], x_ref, 0), (copies[2], grads_ref, width)):
        copy.wait()
        for i in range(ref.shape[0]):
            block[levels * i : levels * (i + 1), low : low + width] = ref[i].astype(jnp.float32)
    out_ref[...] = block[...].astype(jnp.bfloat16)


def fetch_kernel(w_qkv_hbm, w_out_hbm, *refs):
    *targets, sems = refs
    width = w_out_hbm.shape[1]
    copies = []
    for k, target in enumerate(targets):
        source = w_qkv_hbm.at[:, k * width : (k + 1) * width] if k < 3 else w_out_hbm
        copies.append(pltpu.make_async_copy(source, target, sems.at[k]))
    for copy in copies:
        copy.start()
    for copy in copies:
        copy.wait()


def reorder_kernel(in_ref, out_ref, before, after):
    levels = before.shape[0] // (WLAT * WLON)
    before[...] = in_ref[...].astype(jnp.float32)
    for r in range(WLAT):
        for c in range(WLON):
            low, to = levels * (r * WLON + c), levels * (c * WLAT + r)
            after[to : to + levels, :] = before[low : low + levels, :]
    out_ref[...] = after[...].astype(jnp.bfloat16)


def window_kernel(
    shift_ref, both_ref, w_query_ref, w_key_ref, w_value_ref, w_out_ref,
    out_ref, joined_ref, *, lat_count,
):
    tokens, width = out_ref.shape
    head = width // HEADS
    inv_root = 1.0 / head**0.5
    lanes = GROUP * head
    levels = tokens // (WLAT * WLON)
    widened = both_ref[:, :width].astype(jnp.float32)
    centered = widened - jnp.mean(widened, axis=-1, keepdims=True)
    inv_std = lax.rsqrt(jnp.mean(centered * centered, axis=-1, keepdims=True) + EPSILON)
    normed = centered * inv_std
    grads = both_ref[:, width:]
    grad_heads = dot(grads, w_out_ref[...], 1, 1).astype(jnp.bfloat16)
    weights = (w_query_ref, w_key_ref, w_value_ref)
    normed_bf16 = normed.astype(jnp.bfloat16)
    qkv = [dot(normed_bf16, w_ref[...], 1, 0).astype(jnp.bfloat16) for w_ref in weights]

    lat_shift = shift_ref[:1, :1]
    edge = jnp.where(2 * lat_shift >= WLAT, 0, lat_count - 1)
    line = WLAT * levels
    cut = jnp.where(lax.axis_index("lat") == edge, lat_shift * levels, line)

    def place_in_column(at, count):
        start = jnp.zeros_like(at)
        for c in range(1, count // line):
            start = jnp.where(at >= c * line, c * line, start)
        return at - start

    key_at = place_in_column(lax.broadcasted_iota(jnp.int32, (tokens, 1), 0), tokens)
    lane = lax.broadcasted_iota(jnp.int32, (1, GROUP * tokens), 1)
    query_at = place_in_column(lane, GROUP * tokens)
    key_side = jnp.where(key_at >= cut, 1.0, 0.0)
    query_side = jnp.where(query_at >= cut, 1.0, 0.0)
    allowed = key_side == query_side
    lane_head = lax.broadcasted_iota(jnp.int32, (tokens, lanes), 1) // head

    def stack(values):
        return jnp.concatenate(
            [jnp.where(lane_head == h, values, jnp.zeros_like(values)) for h in range(GROUP)],
            axis=0,
        )

    for group in range(HEADS // GROUP):
        low = group * lanes
        queries, keys_all, values_all = (part[:, low : low + lanes] for part in qkv)
        query_stack = stack(queries)
        grad_stack = stack(grad_heads[:, low : low + lanes])
        scores = dot(keys_all, query_stack, 1, 1) * inv_root
        weights_exp = jnp.where(allowed, jnp.exp(scores), 0.0)
        probability = weights_exp * (1.0 / jnp.sum(weights_exp, axis=0, keepdims=True))
        d_probability = dot(values_all, grad_stack, 1, 1)
        delta = jnp.sum(probability * d_probability, axis=0, keepdims=True)
        d_scores = (probability * (d_probability - delta)).astype(jnp.bfloat16)
        d_values = dot(probability.astype(jnp.bfloat16), grad_stack, 1, 0)
        d_keys = dot(d_scores, query_stack, 1, 0) * inv_root
        spread = dot(d_scores, keys_all, 0, 0)
        d_queries = jnp.zeros((tokens, lanes), jnp.float32)
        for h in range(GROUP):
            d_queries = jnp.where(lane_head == h, spread[h * tokens : (h + 1) * tokens], d_queries)
        d_queries = d_queries * inv_root
        joined_ref[:, low : low + lanes] = d_queries.astype(jnp.bfloat16)
        joined_ref[:, width + low : width + low + lanes] = d_keys.astype(jnp.bfloat16)
        joined_ref[:, 2 * width + low : 2 * width + low + lanes] = d_values.astype(jnp.bfloat16)
    d_normed = sum(
        dot(joined_ref[:, k * width : (k + 1) * width], w_ref[...], 1, 1)
        for k, w_ref in enumerate(weights)
    )
    branch = inv_std * (
        d_normed
        - jnp.mean(d_normed, axis=-1, keepdims=True)
        - normed * jnp.mean(d_normed * normed, axis=-1, keepdims=True)
    )
    out_ref[...] = (grads.astype(jnp.float32) + branch).astype(jnp.bfloat16)


def part_kernel(shift_ref, in_ref, kept_ref, upper_ref, lower_ref, before, after):
    tokens = in_ref.shape[0]
    levels, line = tokens // (WLAT * WLON), tokens // WLAT
    before[...] = in_ref[...].astype(jnp.float32)
    for r in range(WLAT):
        for c in range(WLON):
            low, to = levels * (c * WLAT + r), levels * (r * WLON + c)
            after[to : to + levels, :] = before[low : low + levels, :]
    lat_shift = shift_ref[:1, :1]
    cut = lat_shift * line
    ahead = 2 * lat_shift >= WLAT
    at = lax.broadcasted_iota(jnp.int32, (tokens, 1), 0)
    moved = jnp.where(ahead, at - cut, cut - 1 - at) >= 0
    values = after[...]
    zero = jnp.zeros_like(values)
    kept_ref[...] = jnp.where(moved, zero, values).astype(jnp.bfloat16)
    gone = jnp.where(moved, values, zero).astype(jnp.bfloat16)
    upper_ref[...] = gone[tokens - upper_ref.shape[0] :]
    lower_ref[...] = gone[: lower_ref.shape[0]]


def join_kernel(kept_ref, upper_ref, lower_ref, out_hbm, sums, slabs, sems):
    tokens = kept_ref.shape[0]
    levels = slabs.shape[1]
    low, high = lower_ref.shape[0], tokens - upper_ref.shape[0]
    sums[...] = kept_ref[...].astype(jnp.float32)
    sums[:low, :] += lower_ref[...].astype(jnp.float32)
    sums[high:, :] += upper_ref[...].astype(jnp.float32)
    copies = []
    count = slabs.shape[0] // 2
    for k in range(2):
        for i in range(k * count, (k + 1) * count):
            slabs[i] = sums[levels * i : levels * (i + 1), :].astype(jnp.bfloat16)
        half = pl.ds(k * count, count)
        copies.append(pltpu.make_async_copy(slabs.at[half], out_hbm.at[half], sems.at[k]))
        copies[-1].start()
    for copy in copies:
        copy.wait()


def local(block_inputs, out_grads, offsets, w_qkv, w_out):
    _, levels, rows, cols, width = block_inputs.shape
    tokens = levels * rows * cols
    flat = (rows * cols, levels, width)
    vmem = pl.BlockSpec(memory_space=pltpu.VMEM)
    smem = pl.BlockSpec(memory_space=pltpu.SMEM)
    both = (tokens, 2 * width)

    def held(*values):
        return [pltpu.with_memory_space_constraint(value, pltpu.VMEM) for value in values]

    hbm = pl.BlockSpec(memory_space=pl.ANY)
    lat_branch, lon_branch, lat_shift, block = pl.pallas_call(
        pack_kernel,
        out_shape=(
            pltpu.SMEM((1,), jnp.int32),
            pltpu.SMEM((1,), jnp.int32),
            pltpu.VMEM((8, 128), jnp.int32),
            pltpu.VMEM(both, jnp.bfloat16),
        ),
        in_specs=[hbm] * 3,
        out_specs=(smem, smem, vmem, vmem),
        scratch_shapes=[
            pltpu.SMEM(offsets.shape, jnp.int32),
            pltpu.VMEM(flat, jnp.bfloat16),
            pltpu.VMEM(flat, jnp.bfloat16),
            pltpu.VMEM(both, jnp.float32),
            pltpu.SemaphoreType.DMA((3,)),
        ],
        name="pack",
    )(
        offsets,
        block_inputs[0].transpose(1, 2, 0, 3).reshape(flat),
        out_grads[0].transpose(1, 2, 0, 3).reshape(flat),
    )
    lat_branch, lon_branch = lat_branch[0], lon_branch[0]
    (block,) = exchange_by(lat_branch, rows, block, "lat", False)
    block = pl.pallas_call(
        reorder_kernel,
        out_shape=pltpu.VMEM(both, jnp.bfloat16),
        in_specs=[vmem],
        out_specs=vmem,
        scratch_shapes=[pltpu.VMEM(both, jnp.float32)] * 2,
        name="reorder",
    )(*held(block))
    block, *weights = exchange_by(
        lon_branch, cols, block, "lon", False, (w_qkv[0], w_out[0])
    )
    result = pl.pallas_call(
        functools.partial(window_kernel, lat_count=lax.axis_size("lat")),
        out_shape=pltpu.VMEM((tokens, width), jnp.bfloat16),
        in_specs=[vmem] * 6,
        out_specs=vmem,
        scratch_shapes=[pltpu.VMEM((tokens, 3 * width), jnp.bfloat16)],
        name="window",
    )(*held(lat_shift, block, *weights))
    (result,) = exchange_by(lon_branch, cols, result, "lon", True)

    line = tokens // rows
    counts = (tokens, rows // 2 * line, (rows // 2 - 1) * line)
    kept, upper, lower = pl.pallas_call(
        part_kernel,
        out_shape=tuple(pltpu.VMEM((count, width), jnp.bfloat16) for count in counts),
        in_specs=[vmem] * 2,
        out_specs=(vmem,) * 3,
        scratch_shapes=[pltpu.VMEM((tokens, width), jnp.float32)] * 2,
        name="part",
    )(*held(lat_shift, result))
    kept = shift(kept, section=-1)
    upper = shift(upper, section=-1, lat=-1)
    lower = shift(lower, section=-1, lat=1)
    joined = pl.pallas_call(
        join_kernel,
        out_shape=jax.ShapeDtypeStruct(flat, jnp.bfloat16),
        in_specs=[vmem] * 3,
        out_specs=hbm,
        scratch_shapes=[
            pltpu.VMEM((tokens, width), jnp.float32),
            pltpu.VMEM(flat, jnp.bfloat16),
            pltpu.SemaphoreType.DMA((2,)),
        ],
        name="join",
    )(*held(kept, upper, lower))
    return joined.reshape(rows, cols, levels, width).transpose(2, 0, 1, 3)[None]


def solution(mesh):
    return jax.shard_map(
        local,
        mesh=mesh,
        in_specs=(
            P("section", None, "lat", "lon", None),
            P("section", None, "lat", "lon", None),
            P("section", None),
            P("section", None, None),
            P("section", None, None),
        ),
        out_specs=P("section", None, "lat", "lon", None),
        check_vma=False,
    )
```

```python
import functools

import jax
import jax.numpy as jnp
from jax import lax
from jax.experimental import pallas as pl
from jax.experimental.pallas import tpu as pltpu
from jax.sharding import PartitionSpec as P

HEADS = 16
WLAT = 6
WLON = 12
EPSILON = 1e-05
GROUP = 8


def shift(value, **moves):
    axes = tuple(moves)
    pairs = [(0, 0)]
    for axis in axes:
        size, move = lax.axis_size(axis), moves[axis]
        pairs = [
            (s * size + i, d * size + (i + move) % size) for s, d in pairs for i in range(size)
        ]
    return lax.ppermute(value, axes, pairs)


def dot(lhs, rhs, lhs_dim, rhs_dim):
    return lax.dot_general(
        lhs, rhs, (((lhs_dim,), (rhs_dim,)), ((), ())), preferred_element_type=jnp.float32
    )


def exchange(array, axis, cut, size, home):
    forward = 2 * cut >= size
    total = array.shape[0]
    at = cut * (total // size)
    low, high = (at, total) if forward else (0, at)
    strip = shift(array[low:high], **{axis: 1 if forward != home else -1})
    pieces = [array[:at], strip] if forward else [strip, array[at:]]
    return jnp.concatenate(pieces, axis=0)


def exchange_by(branch, size, array, axis, home, weights=()):
    def run(cut):
        def move(value, *weights):
            moved = exchange(value, axis, cut, size, home)
            return moved, *(fetch(*weights) if weights else ())

        return move

    return lax.switch(branch, [run(cut) for cut in range(1, size)], array, *weights)


def send_back(branch, size, array, half):
    line = 2 * half // size

    def run(cut):
        forward = 2 * cut >= size
        low, high = (cut * line - half, half) if forward else (0, cut * line)

        def move(value):
            strip = shift(value[low:high], lat=-1 if forward else 1)
            strip = jnp.pad(strip, ((low, half - high), (0, 0)))
            return jnp.concatenate([strip, value[half:]], axis=0)

        return move

    return lax.switch(branch, [run(cut) for cut in range(1, size)], array)


def fetch(w_qkv, w_out):
    return pl.pallas_call(
        fetch_kernel,
        out_shape=(pltpu.VMEM(w_out.shape, w_out.dtype),) * 4,
        in_specs=[pl.BlockSpec(memory_space=pl.ANY)] * 2,
        out_specs=(pl.BlockSpec(memory_space=pltpu.VMEM),) * 4,
        scratch_shapes=[pltpu.SemaphoreType.DMA((4,))],
        name="fetch",
    )(*(pltpu.with_memory_space_constraint(w, pltpu.HBM) for w in (w_qkv, w_out)))


def pack_kernel(
    offsets_hbm, x_hbm, grads_hbm, lat_branch_ref, lon_branch_ref, shift_ref, out_ref,
    offsets_ref, x_ref, grads_ref, block, sems,
):
    copies = [
        pltpu.make_async_copy(source, target, sems.at[k])
        for k, (source, target) in enumerate(
            ((offsets_hbm, offsets_ref), (x_hbm, x_ref), (grads_hbm, grads_ref))
        )
    ]
    for copy in copies:
        copy.start()
    levels, width = x_ref.shape[1:]
    copies[0].wait()
    lat_branch_ref[0] = offsets_ref[0, 0] - 1
    lon_branch_ref[0] = offsets_ref[0, 1] - 1
    shift_ref[...] = jnp.full(shift_ref.shape, offsets_ref[0, 0], jnp.int32)
    for copy, ref, low in ((copies[1], x_ref, 0), (copies[2], grads_ref, width)):
        copy.wait()
        for i in range(ref.shape[0]):
            block[levels * i : levels * (i + 1), low : low + width] = ref[i].astype(jnp.float32)
    out_ref[...] = block[...].astype(jnp.bfloat16)


def fetch_kernel(w_qkv_hbm, w_out_hbm, *refs):
    *targets, sems = refs
    width = w_out_hbm.shape[1]
    copies = []
    for k, target in enumerate(targets):
        source = w_qkv_hbm.at[:, k * width : (k + 1) * width] if k < 3 else w_out_hbm
        copies.append(pltpu.make_async_copy(source, target, sems.at[k]))
    for copy in copies:
        copy.start()
    for copy in copies:
        copy.wait()


def reorder_kernel(in_ref, out_ref, before, after):
    levels = before.shape[0] // (WLAT * WLON)
    before[...] = in_ref[...].astype(jnp.float32)
    for r in range(WLAT):
        for c in range(WLON):
            low, to = levels * (r * WLON + c), levels * (c * WLAT + r)
            after[to : to + levels, :] = before[low : low + levels, :]
    out_ref[...] = after[...].astype(jnp.bfloat16)


def window_kernel(
    shift_ref, both_ref, w_query_ref, w_key_ref, w_value_ref, w_out_ref,
    out_ref, joined_ref, *, lat_count,
):
    tokens, width = out_ref.shape
    head = width // HEADS
    inv_root = 1.0 / head**0.5
    lanes = GROUP * head
    levels = tokens // (WLAT * WLON)
    widened = both_ref[:, :width].astype(jnp.float32)
    centered = widened - jnp.mean(widened, axis=-1, keepdims=True)
    inv_std = lax.rsqrt(jnp.mean(centered * centered, axis=-1, keepdims=True) + EPSILON)
    normed = centered * inv_std
    grads = both_ref[:, width:]
    grad_heads = dot(grads, w_out_ref[...], 1, 1).astype(jnp.bfloat16)
    weights = (w_query_ref, w_key_ref, w_value_ref)
    normed_bf16 = normed.astype(jnp.bfloat16)
    qkv = [dot(normed_bf16, w_ref[...], 1, 0).astype(jnp.bfloat16) for w_ref in weights]

    lat_shift = shift_ref[:1, :1]
    edge = jnp.where(2 * lat_shift >= WLAT, 0, lat_count - 1)
    line = WLAT * levels
    cut = jnp.where(lax.axis_index("lat") == edge, lat_shift * levels, line)

    def place_in_column(at, count):
        start = jnp.zeros_like(at)
        for c in range(1, count // line):
            start = jnp.where(at >= c * line, c * line, start)
        return at - start

    key_at = place_in_column(lax.broadcasted_iota(jnp.int32, (tokens, 1), 0), tokens)
    lane = lax.broadcasted_iota(jnp.int32, (1, GROUP * tokens), 1)
    query_at = place_in_column(lane, GROUP * tokens)
    key_side = jnp.where(key_at >= cut, 1.0, 0.0)
    query_side = jnp.where(query_at >= cut, 1.0, 0.0)
    allowed = key_side == query_side
    lane_head = lax.broadcasted_iota(jnp.int32, (tokens, lanes), 1) // head

    def stack(values):
        return jnp.concatenate(
            [jnp.where(lane_head == h, values, jnp.zeros_like(values)) for h in range(GROUP)],
            axis=0,
        )

    for group in range(HEADS // GROUP):
        low = group * lanes
        queries, keys_all, values_all = (part[:, low : low + lanes] for part in qkv)
        query_stack = stack(queries)
        grad_stack = stack(grad_heads[:, low : low + lanes])
        scores = dot(keys_all, query_stack, 1, 1) * inv_root
        weights_exp = jnp.where(allowed, jnp.exp(scores), 0.0)
        probability = weights_exp * (1.0 / jnp.sum(weights_exp, axis=0, keepdims=True))
        d_probability = dot(values_all, grad_stack, 1, 1)
        delta = jnp.sum(probability * d_probability, axis=0, keepdims=True)
        d_scores = (probability * (d_probability - delta)).astype(jnp.bfloat16)
        d_values = dot(probability.astype(jnp.bfloat16), grad_stack, 1, 0)
        d_keys = dot(d_scores, query_stack, 1, 0) * inv_root
        spread = dot(d_scores, keys_all, 0, 0)
        d_queries = jnp.zeros((tokens, lanes), jnp.float32)
        for h in range(GROUP):
            d_queries = jnp.where(lane_head == h, spread[h * tokens : (h + 1) * tokens], d_queries)
        d_queries = d_queries * inv_root
        joined_ref[:, low : low + lanes] = d_queries.astype(jnp.bfloat16)
        joined_ref[:, width + low : width + low + lanes] = d_keys.astype(jnp.bfloat16)
        joined_ref[:, 2 * width + low : 2 * width + low + lanes] = d_values.astype(jnp.bfloat16)
    d_normed = sum(
        dot(joined_ref[:, k * width : (k + 1) * width], w_ref[...], 1, 1)
        for k, w_ref in enumerate(weights)
    )
    branch = inv_std * (
        d_normed
        - jnp.mean(d_normed, axis=-1, keepdims=True)
        - normed * jnp.mean(d_normed * normed, axis=-1, keepdims=True)
    )
    out_ref[...] = (grads.astype(jnp.float32) + branch).astype(jnp.bfloat16)


def part_kernel(shift_ref, in_ref, kept_ref, moved_ref, before, after):
    tokens = in_ref.shape[0]
    levels, line, half = tokens // (WLAT * WLON), tokens // WLAT, tokens // 2
    before[...] = in_ref[...].astype(jnp.float32)
    for r in range(WLAT):
        for c in range(WLON):
            low, to = levels * (c * WLAT + r), levels * (r * WLON + c)
            after[to : to + levels, :] = before[low : low + levels, :]
    lat_shift = shift_ref[:1, :1]
    cut = lat_shift * line
    ahead = 2 * lat_shift >= WLAT
    at = lax.broadcasted_iota(jnp.int32, (tokens, 1), 0)
    moved = jnp.where(ahead, at - cut, cut - 1 - at) >= 0
    values = after[...]
    kept_ref[...] = jnp.where(moved, jnp.zeros_like(values), values).astype(jnp.bfloat16)
    part = jnp.where(ahead, values[half:], values[:half])
    flags = moved_ref.shape[0] - half
    flag = jnp.broadcast_to(lat_shift.astype(jnp.float32), (flags, part.shape[1]))
    moved_ref[...] = jnp.concatenate([part, flag], axis=0).astype(jnp.bfloat16)


def join_kernel(kept_ref, moved_ref, out_hbm, sums, slabs, sems):
    tokens = kept_ref.shape[0]
    half = tokens // 2
    levels = slabs.shape[1]
    part = moved_ref[...].astype(jnp.float32)
    ahead = 2.0 * part[half : half + 1, :] >= WLAT
    part = part[:half]
    kept = kept_ref[...].astype(jnp.float32)
    zero = jnp.zeros_like(part)
    sums[:half, :] = kept[:half] + jnp.where(ahead, zero, part)
    sums[half:, :] = kept[half:] + jnp.where(ahead, part, zero)
    copies = []
    count = slabs.shape[0] // 2
    for k in range(2):
        for i in range(k * count, (k + 1) * count):
            slabs[i] = sums[levels * i : levels * (i + 1), :].astype(jnp.bfloat16)
        span = pl.ds(k * count, count)
        copies.append(pltpu.make_async_copy(slabs.at[span], out_hbm.at[span], sems.at[k]))
        copies[-1].start()
    for copy in copies:
        copy.wait()


def local(block_inputs, out_grads, offsets, w_qkv, w_out):
    _, levels, rows, cols, width = block_inputs.shape
    tokens = levels * rows * cols
    flat = (rows * cols, levels, width)
    vmem = pl.BlockSpec(memory_space=pltpu.VMEM)
    smem = pl.BlockSpec(memory_space=pltpu.SMEM)
    both = (tokens, 2 * width)

    def held(*values):
        return [pltpu.with_memory_space_constraint(value, pltpu.VMEM) for value in values]

    hbm = pl.BlockSpec(memory_space=pl.ANY)
    lat_branch, lon_branch, lat_shift, block = pl.pallas_call(
        pack_kernel,
        out_shape=(
            pltpu.SMEM((1,), jnp.int32),
            pltpu.SMEM((1,), jnp.int32),
            pltpu.VMEM((8, 128), jnp.int32),
            pltpu.VMEM(both, jnp.bfloat16),
        ),
        in_specs=[hbm] * 3,
        out_specs=(smem, smem, vmem, vmem),
        scratch_shapes=[
            pltpu.SMEM(offsets.shape, jnp.int32),
            pltpu.VMEM(flat, jnp.bfloat16),
            pltpu.VMEM(flat, jnp.bfloat16),
            pltpu.VMEM(both, jnp.float32),
            pltpu.SemaphoreType.DMA((3,)),
        ],
        name="pack",
    )(
        offsets,
        block_inputs[0].transpose(1, 2, 0, 3).reshape(flat),
        out_grads[0].transpose(1, 2, 0, 3).reshape(flat),
    )
    lat_branch, lon_branch = lat_branch[0], lon_branch[0]
    (block,) = exchange_by(lat_branch, rows, block, "lat", False)
    block = pl.pallas_call(
        reorder_kernel,
        out_shape=pltpu.VMEM(both, jnp.bfloat16),
        in_specs=[vmem],
        out_specs=vmem,
        scratch_shapes=[pltpu.VMEM(both, jnp.float32)] * 2,
        name="reorder",
    )(*held(block))
    block, *weights = exchange_by(
        lon_branch, cols, block, "lon", False, (w_qkv[0], w_out[0])
    )
    result = pl.pallas_call(
        functools.partial(window_kernel, lat_count=lax.axis_size("lat")),
        out_shape=pltpu.VMEM((tokens, width), jnp.bfloat16),
        in_specs=[vmem] * 6,
        out_specs=vmem,
        scratch_shapes=[pltpu.VMEM((tokens, 3 * width), jnp.bfloat16)],
        name="window",
    )(*held(lat_shift, block, *weights))
    (result,) = exchange_by(lon_branch, cols, result, "lon", True)

    half, flags = tokens // 2, 8
    kept, moved = pl.pallas_call(
        part_kernel,
        out_shape=(
            pltpu.VMEM((tokens, width), jnp.bfloat16),
            pltpu.VMEM((half + flags, width), jnp.bfloat16),
        ),
        in_specs=[vmem] * 2,
        out_specs=(vmem,) * 2,
        scratch_shapes=[pltpu.VMEM((tokens, width), jnp.float32)] * 2,
        name="part",
    )(*held(lat_shift, result))
    kept = shift(kept, section=-1)
    moved = send_back(lat_branch, rows, moved, half)
    moved = shift(moved, section=-1)
    joined = pl.pallas_call(
        join_kernel,
        out_shape=jax.ShapeDtypeStruct(flat, jnp.bfloat16),
        in_specs=[vmem] * 2,
        out_specs=hbm,
        scratch_shapes=[
            pltpu.VMEM((tokens, width), jnp.float32),
            pltpu.VMEM(flat, jnp.bfloat16),
            pltpu.SemaphoreType.DMA((2,)),
        ],
        name="join",
    )(*held(kept, moved))
    return joined.reshape(rows, cols, levels, width).transpose(2, 0, 1, 3)[None]


def solution(mesh):
    return jax.shard_map(
        local,
        mesh=mesh,
        in_specs=(
            P("section", None, "lat", "lon", None),
            P("section", None, "lat", "lon", None),
            P("section", None),
            P("section", None, None),
            P("section", None, None),
        ),
        out_specs=P("section", None, "lat", "lon", None),
        check_vma=False,
    )
```

```python
import functools

import jax
import jax.numpy as jnp
from jax import lax
from jax.experimental import pallas as pl
from jax.experimental.pallas import tpu as pltpu
from jax.sharding import PartitionSpec as P

HEADS = 16
WLAT = 6
WLON = 12
EPSILON = 1e-05
GROUP = 4
AHEAD_FROM = {"lat": 3, "lon": 4}


def shift(value, **moves):
    axes = tuple(moves)
    pairs = [(0, 0)]
    for axis in axes:
        size, move = lax.axis_size(axis), moves[axis]
        pairs = [
            (s * size + i, d * size + (i + move) % size) for s, d in pairs for i in range(size)
        ]
    return lax.ppermute(value, axes, pairs)


def dot(lhs, rhs, lhs_dim, rhs_dim):
    return lax.dot_general(
        lhs, rhs, (((lhs_dim,), (rhs_dim,)), ((), ())), preferred_element_type=jnp.float32
    )


def exchange(array, axis, cut, size, home):
    forward = cut >= AHEAD_FROM[axis]
    total = array.shape[0]
    at = cut * (total // size)
    low, high = (at, total) if forward else (0, at)
    strip = shift(array[low:high], **{axis: 1 if forward != home else -1})
    pieces = [array[:at], strip] if forward else [strip, array[at:]]
    return jnp.concatenate(pieces, axis=0)


def exchange_by(branch, size, array, axis, home, weights=()):
    def run(cut):
        def move(value, *weights):
            moved = exchange(value, axis, cut, size, home)
            return moved, *(fetch(*weights) if weights else ())

        return move

    return lax.switch(branch, [run(cut) for cut in range(1, size)], array, *weights)


def fetch(w_qkv, w_out):
    return pl.pallas_call(
        fetch_kernel,
        out_shape=(pltpu.VMEM(w_out.shape, w_out.dtype),) * 4,
        in_specs=[pl.BlockSpec(memory_space=pl.ANY)] * 2,
        out_specs=(pl.BlockSpec(memory_space=pltpu.VMEM),) * 4,
        scratch_shapes=[pltpu.SemaphoreType.DMA((4,))],
        name="fetch",
    )(*(pltpu.with_memory_space_constraint(w, pltpu.HBM) for w in (w_qkv, w_out)))


def pack_kernel(
    offsets_hbm, x_hbm, grads_hbm, lat_branch_ref, lon_branch_ref, shift_ref, out_ref,
    offsets_ref, x_ref, grads_ref, block, sems,
):
    copies = [
        pltpu.make_async_copy(source, target, sems.at[k])
        for k, (source, target) in enumerate(
            ((offsets_hbm, offsets_ref), (x_hbm, x_ref), (grads_hbm, grads_ref))
        )
    ]
    for copy in copies:
        copy.start()
    levels, width = x_ref.shape[1:]
    copies[0].wait()
    lat_branch_ref[0] = offsets_ref[0, 0] - 1
    lon_branch_ref[0] = offsets_ref[0, 1] - 1
    shift_ref[...] = jnp.full(shift_ref.shape, offsets_ref[0, 0], jnp.int32)
    for copy, ref, low in ((copies[1], x_ref, 0), (copies[2], grads_ref, width)):
        copy.wait()
        for i in range(ref.shape[0]):
            block[levels * i : levels * (i + 1), low : low + width] = ref[i].astype(jnp.float32)
    out_ref[...] = block[...].astype(jnp.bfloat16)


def fetch_kernel(w_qkv_hbm, w_out_hbm, *refs):
    *targets, sems = refs
    width = w_out_hbm.shape[1]
    copies = []
    for k, target in enumerate(targets):
        source = w_qkv_hbm.at[:, k * width : (k + 1) * width] if k < 3 else w_out_hbm
        copies.append(pltpu.make_async_copy(source, target, sems.at[k]))
    for copy in copies:
        copy.start()
    for copy in copies:
        copy.wait()


def reorder_kernel(in_ref, out_ref, before, after):
    levels = before.shape[0] // (WLAT * WLON)
    before[...] = in_ref[...].astype(jnp.float32)
    for r in range(WLAT):
        for c in range(WLON):
            low, to = levels * (r * WLON + c), levels * (c * WLAT + r)
            after[to : to + levels, :] = before[low : low + levels, :]
    out_ref[...] = after[...].astype(jnp.bfloat16)


def window_kernel(
    shift_ref, both_ref, w_query_ref, w_key_ref, w_value_ref, w_out_ref,
    out_ref, joined_ref, *, lat_count,
):
    tokens, width = out_ref.shape
    head = width // HEADS
    inv_root = 1.0 / head**0.5
    lanes = GROUP * head
    levels = tokens // (WLAT * WLON)
    widened = both_ref[:, :width].astype(jnp.float32)
    centered = widened - jnp.mean(widened, axis=-1, keepdims=True)
    inv_std = lax.rsqrt(jnp.mean(centered * centered, axis=-1, keepdims=True) + EPSILON)
    normed = centered * inv_std
    grads = both_ref[:, width:]
    grad_heads = dot(grads, w_out_ref[...], 1, 1).astype(jnp.bfloat16)
    weights = (w_query_ref, w_key_ref, w_value_ref)
    normed_bf16 = normed.astype(jnp.bfloat16)
    w_qkv = jnp.concatenate([w_ref[...] for w_ref in weights], axis=1)
    joined = dot(normed_bf16, w_qkv, 1, 0).astype(jnp.bfloat16)
    qkv = [joined[:, k * width : (k + 1) * width] for k in range(3)]

    lat_shift = shift_ref[:1, :1]
    edge = jnp.where(lat_shift >= AHEAD_FROM["lat"], 0, lat_count - 1)
    line = WLAT * levels
    cut = jnp.where(lax.axis_index("lat") == edge, lat_shift * levels, line)

    def place_in_column(at, count):
        start = jnp.zeros_like(at)
        for c in range(1, count // line):
            start = jnp.where(at >= c * line, c * line, start)
        return at - start

    key_at = place_in_column(lax.broadcasted_iota(jnp.int32, (tokens, 1), 0), tokens)
    lane = lax.broadcasted_iota(jnp.int32, (1, GROUP * tokens), 1)
    query_at = place_in_column(lane, GROUP * tokens)
    key_side = jnp.where(key_at >= cut, 1.0, 0.0)
    query_side = jnp.where(query_at >= cut, 1.0, 0.0)
    allowed = key_side == query_side
    lane_head = lax.broadcasted_iota(jnp.int32, (tokens, lanes), 1) // head

    def stack(values):
        return jnp.concatenate(
            [jnp.where(lane_head == h, values, jnp.zeros_like(values)) for h in range(GROUP)],
            axis=0,
        )

    for group in range(HEADS // GROUP):
        low = group * lanes
        queries, keys_all, values_all = (part[:, low : low + lanes] for part in qkv)
        query_stack = stack(queries)
        grad_stack = stack(grad_heads[:, low : low + lanes])
        scores = dot(keys_all, query_stack, 1, 1) * inv_root
        weights_exp = jnp.where(allowed, jnp.exp(scores), 0.0)
        probability = weights_exp * (1.0 / jnp.sum(weights_exp, axis=0, keepdims=True))
        d_probability = dot(values_all, grad_stack, 1, 1)
        delta = jnp.sum(probability * d_probability, axis=0, keepdims=True)
        d_scores = (probability * (d_probability - delta)).astype(jnp.bfloat16)
        d_values = dot(probability.astype(jnp.bfloat16), grad_stack, 1, 0)
        d_keys = dot(d_scores, query_stack, 1, 0) * inv_root
        spread = dot(d_scores, keys_all, 0, 0)
        d_queries = jnp.zeros((tokens, lanes), jnp.float32)
        for h in range(GROUP):
            d_queries = jnp.where(lane_head == h, spread[h * tokens : (h + 1) * tokens], d_queries)
        d_queries = d_queries * inv_root
        joined_ref[:, low : low + lanes] = d_queries.astype(jnp.bfloat16)
        joined_ref[:, width + low : width + low + lanes] = d_keys.astype(jnp.bfloat16)
        joined_ref[:, 2 * width + low : 2 * width + low + lanes] = d_values.astype(jnp.bfloat16)
    d_normed = dot(joined_ref[...], w_qkv, 1, 1)
    branch = inv_std * (
        d_normed
        - jnp.mean(d_normed, axis=-1, keepdims=True)
        - normed * jnp.mean(d_normed * normed, axis=-1, keepdims=True)
    )
    out_ref[...] = (grads.astype(jnp.float32) + branch).astype(jnp.bfloat16)


def part_kernel(shift_ref, in_ref, kept_ref, upper_ref, lower_ref, before, after):
    tokens = in_ref.shape[0]
    levels, line = tokens // (WLAT * WLON), tokens // WLAT
    before[...] = in_ref[...].astype(jnp.float32)
    for r in range(WLAT):
        for c in range(WLON):
            low, to = levels * (c * WLAT + r), levels * (r * WLON + c)
            after[to : to + levels, :] = before[low : low + levels, :]
    lat_shift = shift_ref[:1, :1]
    cut = lat_shift * line
    ahead = lat_shift >= AHEAD_FROM["lat"]
    at = lax.broadcasted_iota(jnp.int32, (tokens, 1), 0)
    moved = jnp.where(ahead, at - cut, cut - 1 - at) >= 0
    values = after[...]
    zero = jnp.zeros_like(values)
    kept_ref[...] = jnp.where(moved, zero, values).astype(jnp.bfloat16)
    gone = jnp.where(moved, values, zero).astype(jnp.bfloat16)
    upper_ref[...] = gone[tokens - upper_ref.shape[0] :]
    lower_ref[...] = gone[: lower_ref.shape[0]]


def join_kernel(kept_ref, upper_ref, lower_ref, out_hbm, sums, slabs, sems):
    tokens = kept_ref.shape[0]
    levels = slabs.shape[1]
    low, high = lower_ref.shape[0], tokens - upper_ref.shape[0]
    sums[...] = kept_ref[...].astype(jnp.float32)
    sums[:low, :] += lower_ref[...].astype(jnp.float32)
    sums[high:, :] += upper_ref[...].astype(jnp.float32)
    copies = []
    count = slabs.shape[0] // 2
    for k in range(2):
        for i in range(k * count, (k + 1) * count):
            slabs[i] = sums[levels * i : levels * (i + 1), :].astype(jnp.bfloat16)
        half = pl.ds(k * count, count)
        copies.append(pltpu.make_async_copy(slabs.at[half], out_hbm.at[half], sems.at[k]))
        copies[-1].start()
    for copy in copies:
        copy.wait()


def local(block_inputs, out_grads, offsets, w_qkv, w_out):
    _, levels, rows, cols, width = block_inputs.shape
    tokens = levels * rows * cols
    flat = (rows * cols, levels, width)
    vmem = pl.BlockSpec(memory_space=pltpu.VMEM)
    smem = pl.BlockSpec(memory_space=pltpu.SMEM)
    both = (tokens, 2 * width)

    def held(*values):
        return [pltpu.with_memory_space_constraint(value, pltpu.VMEM) for value in values]

    hbm = pl.BlockSpec(memory_space=pl.ANY)
    lat_branch, lon_branch, lat_shift, block = pl.pallas_call(
        pack_kernel,
        out_shape=(
            pltpu.SMEM((1,), jnp.int32),
            pltpu.SMEM((1,), jnp.int32),
            pltpu.VMEM((8, 128), jnp.int32),
            pltpu.VMEM(both, jnp.bfloat16),
        ),
        in_specs=[hbm] * 3,
        out_specs=(smem, smem, vmem, vmem),
        scratch_shapes=[
            pltpu.SMEM(offsets.shape, jnp.int32),
            pltpu.VMEM(flat, jnp.bfloat16),
            pltpu.VMEM(flat, jnp.bfloat16),
            pltpu.VMEM(both, jnp.float32),
            pltpu.SemaphoreType.DMA((3,)),
        ],
        name="pack",
    )(
        offsets,
        block_inputs[0].transpose(1, 2, 0, 3).reshape(flat),
        out_grads[0].transpose(1, 2, 0, 3).reshape(flat),
    )
    lat_branch, lon_branch = lat_branch[0], lon_branch[0]
    (block,) = exchange_by(lat_branch, rows, block, "lat", False)
    block = pl.pallas_call(
        reorder_kernel,
        out_shape=pltpu.VMEM(both, jnp.bfloat16),
        in_specs=[vmem],
        out_specs=vmem,
        scratch_shapes=[pltpu.VMEM(both, jnp.float32)] * 2,
        name="reorder",
    )(*held(block))
    block, *weights = exchange_by(
        lon_branch, cols, block, "lon", False, (w_qkv[0], w_out[0])
    )
    result = pl.pallas_call(
        functools.partial(window_kernel, lat_count=lax.axis_size("lat")),
        out_shape=pltpu.VMEM((tokens, width), jnp.bfloat16),
        in_specs=[vmem] * 6,
        out_specs=vmem,
        scratch_shapes=[pltpu.VMEM((tokens, 3 * width), jnp.bfloat16)],
        name="window",
    )(*held(lat_shift, block, *weights))
    (result,) = exchange_by(lon_branch, cols, result, "lon", True)

    line = tokens // rows
    counts = (tokens, rows // 2 * line, (rows // 2 - 1) * line)
    kept, upper, lower = pl.pallas_call(
        part_kernel,
        out_shape=tuple(pltpu.VMEM((count, width), jnp.bfloat16) for count in counts),
        in_specs=[vmem] * 2,
        out_specs=(vmem,) * 3,
        scratch_shapes=[pltpu.VMEM((tokens, width), jnp.float32)] * 2,
        name="part",
    )(*held(lat_shift, result))
    kept = shift(kept, section=-1)
    upper = shift(upper, section=-1, lat=-1)
    lower = shift(lower, section=-1, lat=1)
    joined = pl.pallas_call(
        join_kernel,
        out_shape=jax.ShapeDtypeStruct(flat, jnp.bfloat16),
        in_specs=[vmem] * 3,
        out_specs=hbm,
        scratch_shapes=[
            pltpu.VMEM((tokens, width), jnp.float32),
            pltpu.VMEM(flat, jnp.bfloat16),
            pltpu.SemaphoreType.DMA((2,)),
        ],
        name="join",
    )(*held(kept, upper, lower))
    return joined.reshape(rows, cols, levels, width).transpose(2, 0, 1, 3)[None]


def solution(mesh):
    return jax.shard_map(
        local,
        mesh=mesh,
        in_specs=(
            P("section", None, "lat", "lon", None),
            P("section", None, "lat", "lon", None),
            P("section", None),
            P("section", None, None),
            P("section", None, None),
        ),
        out_specs=P("section", None, "lat", "lon", None),
        check_vma=False,
    )
```

```python
import functools

import jax
import jax.numpy as jnp
from jax import lax
from jax.experimental import pallas as pl
from jax.experimental.pallas import tpu as pltpu
from jax.sharding import PartitionSpec as P

HEADS = 16
WLAT = 6
WLON = 12
EPSILON = 1e-05
GROUP = 4
AHEAD_FROM = {"lat": WLAT, "lon": 4}


def shift(value, **moves):
    axes = tuple(moves)
    pairs = [(0, 0)]
    for axis in axes:
        size, move = lax.axis_size(axis), moves[axis]
        pairs = [
            (s * size + i, d * size + (i + move) % size) for s, d in pairs for i in range(size)
        ]
    return lax.ppermute(value, axes, pairs)


def dot(lhs, rhs, lhs_dim, rhs_dim):
    return lax.dot_general(
        lhs, rhs, (((lhs_dim,), (rhs_dim,)), ((), ())), preferred_element_type=jnp.float32
    )


def exchange(array, axis, cut, size, home):
    forward = cut >= AHEAD_FROM[axis]
    total = array.shape[0]
    at = cut * (total // size)
    low, high = (at, total) if forward else (0, at)
    strip = shift(array[low:high], **{axis: 1 if forward != home else -1})
    pieces = [array[:at], strip] if forward else [strip, array[at:]]
    return jnp.concatenate(pieces, axis=0)


def exchange_by(branch, size, array, axis, home, weights=()):
    def run(cut):
        def move(value, *weights):
            moved = exchange(value, axis, cut, size, home)
            return moved, *(fetch(*weights) if weights else ())

        return move

    return lax.switch(branch, [run(cut) for cut in range(1, size)], array, *weights)


def fetch(w_qkv, w_out):
    return pl.pallas_call(
        fetch_kernel,
        out_shape=(pltpu.VMEM(w_out.shape, w_out.dtype),) * 4,
        in_specs=[pl.BlockSpec(memory_space=pl.ANY)] * 2,
        out_specs=(pl.BlockSpec(memory_space=pltpu.VMEM),) * 4,
        scratch_shapes=[pltpu.SemaphoreType.DMA((4,))],
        name="fetch",
    )(*(pltpu.with_memory_space_constraint(w, pltpu.HBM) for w in (w_qkv, w_out)))


def pack_kernel(
    offsets_hbm, x_hbm, grads_hbm, lat_branch_ref, lon_branch_ref, shift_ref, out_ref,
    offsets_ref, x_ref, grads_ref, block, sems,
):
    copies = [
        pltpu.make_async_copy(source, target, sems.at[k])
        for k, (source, target) in enumerate(
            ((offsets_hbm, offsets_ref), (x_hbm, x_ref), (grads_hbm, grads_ref))
        )
    ]
    for copy in copies:
        copy.start()
    levels, width = x_ref.shape[1:]
    copies[0].wait()
    lat_branch_ref[0] = offsets_ref[0, 0] - 1
    lon_branch_ref[0] = offsets_ref[0, 1] - 1
    shift_ref[...] = jnp.full(shift_ref.shape, offsets_ref[0, 0], jnp.int32)
    for copy, ref, low in ((copies[1], x_ref, 0), (copies[2], grads_ref, width)):
        copy.wait()
        for i in range(ref.shape[0]):
            block[levels * i : levels * (i + 1), low : low + width] = ref[i].astype(jnp.float32)
    out_ref[...] = block[...].astype(jnp.bfloat16)


def fetch_kernel(w_qkv_hbm, w_out_hbm, *refs):
    *targets, sems = refs
    width = w_out_hbm.shape[1]
    copies = []
    for k, target in enumerate(targets):
        source = w_qkv_hbm.at[:, k * width : (k + 1) * width] if k < 3 else w_out_hbm
        copies.append(pltpu.make_async_copy(source, target, sems.at[k]))
    for copy in copies:
        copy.start()
    for copy in copies:
        copy.wait()


def reorder_kernel(in_ref, out_ref, before, after):
    levels = before.shape[0] // (WLAT * WLON)
    before[...] = in_ref[...].astype(jnp.float32)
    for r in range(WLAT):
        for c in range(WLON):
            low, to = levels * (r * WLON + c), levels * (c * WLAT + r)
            after[to : to + levels, :] = before[low : low + levels, :]
    out_ref[...] = after[...].astype(jnp.bfloat16)


def window_kernel(
    shift_ref, both_ref, w_query_ref, w_key_ref, w_value_ref, w_out_ref,
    out_ref, joined_ref, *, lat_count,
):
    tokens, width = out_ref.shape
    head = width // HEADS
    inv_root = 1.0 / head**0.5
    lanes = GROUP * head
    levels = tokens // (WLAT * WLON)
    widened = both_ref[:, :width].astype(jnp.float32)
    centered = widened - jnp.mean(widened, axis=-1, keepdims=True)
    inv_std = lax.rsqrt(jnp.mean(centered * centered, axis=-1, keepdims=True) + EPSILON)
    normed = centered * inv_std
    grads = both_ref[:, width:]
    grad_heads = dot(grads, w_out_ref[...], 1, 1).astype(jnp.bfloat16)
    weights = (w_query_ref, w_key_ref, w_value_ref)
    normed_bf16 = normed.astype(jnp.bfloat16)
    w_qkv = jnp.concatenate([w_ref[...] for w_ref in weights], axis=1)
    joined = dot(normed_bf16, w_qkv, 1, 0).astype(jnp.bfloat16)
    qkv = [joined[:, k * width : (k + 1) * width] for k in range(3)]

    lat_shift = shift_ref[:1, :1]
    line = WLAT * levels
    cut = jnp.where(lax.axis_index("lat") == lat_count - 1, lat_shift * levels, line)

    def place_in_column(at, count):
        start = jnp.zeros_like(at)
        for c in range(1, count // line):
            start = jnp.where(at >= c * line, c * line, start)
        return at - start

    key_at = place_in_column(lax.broadcasted_iota(jnp.int32, (tokens, 1), 0), tokens)
    lane = lax.broadcasted_iota(jnp.int32, (1, GROUP * tokens), 1)
    query_at = place_in_column(lane, GROUP * tokens)
    key_side = jnp.where(key_at >= cut, 1.0, 0.0)
    query_side = jnp.where(query_at >= cut, 1.0, 0.0)
    allowed = key_side == query_side
    lane_head = lax.broadcasted_iota(jnp.int32, (tokens, lanes), 1) // head

    def stack(values):
        return jnp.concatenate(
            [jnp.where(lane_head == h, values, jnp.zeros_like(values)) for h in range(GROUP)],
            axis=0,
        )

    for group in range(HEADS // GROUP):
        low = group * lanes
        queries, keys_all, values_all = (part[:, low : low + lanes] for part in qkv)
        query_stack = stack(queries)
        grad_stack = stack(grad_heads[:, low : low + lanes])
        scores = dot(keys_all, query_stack, 1, 1) * inv_root
        weights_exp = jnp.where(allowed, jnp.exp(scores), 0.0)
        probability = weights_exp * (1.0 / jnp.sum(weights_exp, axis=0, keepdims=True))
        d_probability = dot(values_all, grad_stack, 1, 1)
        delta = jnp.sum(probability * d_probability, axis=0, keepdims=True)
        d_scores = (probability * (d_probability - delta)).astype(jnp.bfloat16)
        d_values = dot(probability.astype(jnp.bfloat16), grad_stack, 1, 0)
        d_keys = dot(d_scores, query_stack, 1, 0) * inv_root
        spread = dot(d_scores, keys_all, 0, 0)
        d_queries = jnp.zeros((tokens, lanes), jnp.float32)
        for h in range(GROUP):
            d_queries = jnp.where(lane_head == h, spread[h * tokens : (h + 1) * tokens], d_queries)
        d_queries = d_queries * inv_root
        joined_ref[:, low : low + lanes] = d_queries.astype(jnp.bfloat16)
        joined_ref[:, width + low : width + low + lanes] = d_keys.astype(jnp.bfloat16)
        joined_ref[:, 2 * width + low : 2 * width + low + lanes] = d_values.astype(jnp.bfloat16)
    d_normed = dot(joined_ref[...], w_qkv, 1, 1)
    branch = inv_std * (
        d_normed
        - jnp.mean(d_normed, axis=-1, keepdims=True)
        - normed * jnp.mean(d_normed * normed, axis=-1, keepdims=True)
    )
    out_ref[...] = (grads.astype(jnp.float32) + branch).astype(jnp.bfloat16)


def part_kernel(shift_ref, in_ref, kept_ref, moved_ref, before, after):
    tokens = in_ref.shape[0]
    levels, line = tokens // (WLAT * WLON), tokens // WLAT
    before[...] = in_ref[...].astype(jnp.float32)
    for r in range(WLAT):
        for c in range(WLON):
            low, to = levels * (c * WLAT + r), levels * (r * WLON + c)
            after[to : to + levels, :] = before[low : low + levels, :]
    at = lax.broadcasted_iota(jnp.int32, (tokens, 1), 0)
    moved = at < shift_ref[:1, :1] * line
    values = after[...]
    zero = jnp.zeros_like(values)
    kept_ref[...] = jnp.where(moved, zero, values)[line:].astype(jnp.bfloat16)
    moved_ref[...] = jnp.where(moved, values, zero)[: tokens - line].astype(jnp.bfloat16)


def join_kernel(kept_ref, moved_ref, out_hbm, sums, slabs, sems):
    levels = slabs.shape[1]
    tokens = sums.shape[0]
    line = tokens - kept_ref.shape[0]
    moved = moved_ref[...].astype(jnp.float32)
    kept = kept_ref[...].astype(jnp.float32)
    sums[:line, :] = moved[:line]
    sums[line : tokens - line, :] = kept[: tokens - 2 * line] + moved[line:]
    sums[tokens - line :, :] = kept[tokens - 2 * line :]
    copies = []
    count = slabs.shape[0] // 2
    for k in range(2):
        for i in range(k * count, (k + 1) * count):
            slabs[i] = sums[levels * i : levels * (i + 1), :].astype(jnp.bfloat16)
        half = pl.ds(k * count, count)
        copies.append(pltpu.make_async_copy(slabs.at[half], out_hbm.at[half], sems.at[k]))
        copies[-1].start()
    for copy in copies:
        copy.wait()


def local(block_inputs, out_grads, offsets, w_qkv, w_out):
    _, levels, rows, cols, width = block_inputs.shape
    tokens = levels * rows * cols
    flat = (rows * cols, levels, width)
    vmem = pl.BlockSpec(memory_space=pltpu.VMEM)
    smem = pl.BlockSpec(memory_space=pltpu.SMEM)
    both = (tokens, 2 * width)

    def held(*values):
        return [pltpu.with_memory_space_constraint(value, pltpu.VMEM) for value in values]

    hbm = pl.BlockSpec(memory_space=pl.ANY)
    lat_branch, lon_branch, lat_shift, block = pl.pallas_call(
        pack_kernel,
        out_shape=(
            pltpu.SMEM((1,), jnp.int32),
            pltpu.SMEM((1,), jnp.int32),
            pltpu.VMEM((8, 128), jnp.int32),
            pltpu.VMEM(both, jnp.bfloat16),
        ),
        in_specs=[hbm] * 3,
        out_specs=(smem, smem, vmem, vmem),
        scratch_shapes=[
            pltpu.SMEM(offsets.shape, jnp.int32),
            pltpu.VMEM(flat, jnp.bfloat16),
            pltpu.VMEM(flat, jnp.bfloat16),
            pltpu.VMEM(both, jnp.float32),
            pltpu.SemaphoreType.DMA((3,)),
        ],
        name="pack",
    )(
        offsets,
        block_inputs[0].transpose(1, 2, 0, 3).reshape(flat),
        out_grads[0].transpose(1, 2, 0, 3).reshape(flat),
    )
    lat_branch, lon_branch = lat_branch[0], lon_branch[0]
    (block,) = exchange_by(lat_branch, rows, block, "lat", False)
    block = pl.pallas_call(
        reorder_kernel,
        out_shape=pltpu.VMEM(both, jnp.bfloat16),
        in_specs=[vmem],
        out_specs=vmem,
        scratch_shapes=[pltpu.VMEM(both, jnp.float32)] * 2,
        name="reorder",
    )(*held(block))
    block, *weights = exchange_by(
        lon_branch, cols, block, "lon", False, (w_qkv[0], w_out[0])
    )
    result = pl.pallas_call(
        functools.partial(window_kernel, lat_count=lax.axis_size("lat")),
        out_shape=pltpu.VMEM((tokens, width), jnp.bfloat16),
        in_specs=[vmem] * 6,
        out_specs=vmem,
        scratch_shapes=[pltpu.VMEM((tokens, 3 * width), jnp.bfloat16)],
        name="window",
    )(*held(lat_shift, block, *weights))
    (result,) = exchange_by(lon_branch, cols, result, "lon", True)

    rest = pltpu.VMEM((tokens - tokens // rows, width), jnp.bfloat16)
    kept, moved = pl.pallas_call(
        part_kernel,
        out_shape=(rest, rest),
        in_specs=[vmem] * 2,
        out_specs=(vmem,) * 2,
        scratch_shapes=[pltpu.VMEM((tokens, width), jnp.float32)] * 2,
        name="part",
    )(*held(lat_shift, result))
    moved = shift(moved, section=-1, lat=1)
    kept = shift(kept, section=-1)
    joined = pl.pallas_call(
        join_kernel,
        out_shape=jax.ShapeDtypeStruct(flat, jnp.bfloat16),
        in_specs=[vmem] * 2,
        out_specs=hbm,
        scratch_shapes=[
            pltpu.VMEM((tokens, width), jnp.float32),
            pltpu.VMEM(flat, jnp.bfloat16),
            pltpu.SemaphoreType.DMA((2,)),
        ],
        name="join",
    )(*held(kept, moved))
    return joined.reshape(rows, cols, levels, width).transpose(2, 0, 1, 3)[None]


def solution(mesh):
    return jax.shard_map(
        local,
        mesh=mesh,
        in_specs=(
            P("section", None, "lat", "lon", None),
            P("section", None, "lat", "lon", None),
            P("section", None),
            P("section", None, None),
            P("section", None, None),
        ),
        out_specs=P("section", None, "lat", "lon", None),
        check_vma=False,
    )
```

```python
import functools

import jax
import jax.numpy as jnp
from jax import lax
from jax.experimental import pallas as pl
from jax.experimental.pallas import tpu as pltpu
from jax.sharding import PartitionSpec as P

HEADS = 16
WLAT = 6
WLON = 12
EPSILON = 1e-05
GROUP = 4
AHEAD_FROM = {"lat": WLAT, "lon": 3}


def shift(value, **moves):
    axes = tuple(moves)
    pairs = [(0, 0)]
    for axis in axes:
        size, move = lax.axis_size(axis), moves[axis]
        pairs = [
            (s * size + i, d * size + (i + move) % size) for s, d in pairs for i in range(size)
        ]
    return lax.ppermute(value, axes, pairs)


def dot(lhs, rhs, lhs_dim, rhs_dim):
    return lax.dot_general(
        lhs, rhs, (((lhs_dim,), (rhs_dim,)), ((), ())), preferred_element_type=jnp.float32
    )


def exchange(array, axis, cut, size, home):
    forward = cut >= AHEAD_FROM[axis]
    total = array.shape[0]
    at = cut * (total // size)
    low, high = (at, total) if forward else (0, at)
    strip = shift(array[low:high], **{axis: 1 if forward != home else -1})
    pieces = [array[:at], strip] if forward else [strip, array[at:]]
    return jnp.concatenate(pieces, axis=0)


def exchange_by(branch, size, array, axis, home, weights=()):
    def run(cut):
        def move(value, *weights):
            moved = exchange(value, axis, cut, size, home)
            return moved, *(fetch(*weights) if weights else ())

        return move

    return lax.switch(branch, [run(cut) for cut in range(1, size)], array, *weights)


def fetch(w_qkv, w_out):
    return pl.pallas_call(
        fetch_kernel,
        out_shape=(pltpu.VMEM(w_out.shape, w_out.dtype),) * 4,
        in_specs=[pl.BlockSpec(memory_space=pl.ANY)] * 2,
        out_specs=(pl.BlockSpec(memory_space=pltpu.VMEM),) * 4,
        scratch_shapes=[pltpu.SemaphoreType.DMA((4,))],
        name="fetch",
    )(*(pltpu.with_memory_space_constraint(w, pltpu.HBM) for w in (w_qkv, w_out)))


def pack_kernel(
    offsets_hbm, x_hbm, grads_hbm, lat_branch_ref, lon_branch_ref, shift_ref, out_ref,
    offsets_ref, x_ref, grads_ref, block, sems,
):
    copies = [
        pltpu.make_async_copy(source, target, sems.at[k])
        for k, (source, target) in enumerate(
            ((offsets_hbm, offsets_ref), (x_hbm, x_ref), (grads_hbm, grads_ref))
        )
    ]
    for copy in copies:
        copy.start()
    levels, width = x_ref.shape[1:]
    copies[0].wait()
    lat_branch_ref[0] = offsets_ref[0, 0] - 1
    lon_branch_ref[0] = offsets_ref[0, 1] - 1
    shift_ref[...] = jnp.full(shift_ref.shape, offsets_ref[0, 0], jnp.int32)
    for copy, ref, low in ((copies[1], x_ref, 0), (copies[2], grads_ref, width)):
        copy.wait()
        for i in range(ref.shape[0]):
            block[levels * i : levels * (i + 1), low : low + width] = ref[i].astype(jnp.float32)
    out_ref[...] = block[...].astype(jnp.bfloat16)


def fetch_kernel(w_qkv_hbm, w_out_hbm, *refs):
    *targets, sems = refs
    width = w_out_hbm.shape[1]
    copies = []
    for k, target in enumerate(targets):
        source = w_qkv_hbm.at[:, k * width : (k + 1) * width] if k < 3 else w_out_hbm
        copies.append(pltpu.make_async_copy(source, target, sems.at[k]))
    for copy in copies:
        copy.start()
    for copy in copies:
        copy.wait()


def reorder_kernel(in_ref, out_ref, before, after):
    levels = before.shape[0] // (WLAT * WLON)
    before[...] = in_ref[...].astype(jnp.float32)
    for r in range(WLAT):
        for c in range(WLON):
            low, to = levels * (r * WLON + c), levels * (c * WLAT + r)
            after[to : to + levels, :] = before[low : low + levels, :]
    out_ref[...] = after[...].astype(jnp.bfloat16)


def window_kernel(
    shift_ref, both_ref, w_query_ref, w_key_ref, w_value_ref, w_out_ref,
    out_ref, joined_ref, *, lat_count,
):
    tokens, width = out_ref.shape
    head = width // HEADS
    inv_root = 1.0 / head**0.5
    lanes = GROUP * head
    levels = tokens // (WLAT * WLON)
    widened = both_ref[:, :width].astype(jnp.float32)
    centered = widened - jnp.mean(widened, axis=-1, keepdims=True)
    inv_std = lax.rsqrt(jnp.mean(centered * centered, axis=-1, keepdims=True) + EPSILON)
    normed = centered * inv_std
    grads = both_ref[:, width:]
    grad_heads = dot(grads, w_out_ref[...], 1, 1).astype(jnp.bfloat16)
    weights = (w_query_ref, w_key_ref, w_value_ref)
    normed_bf16 = normed.astype(jnp.bfloat16)
    w_qkv = jnp.concatenate([w_ref[...] for w_ref in weights], axis=1)
    joined = dot(normed_bf16, w_qkv, 1, 0).astype(jnp.bfloat16)
    qkv = [joined[:, k * width : (k + 1) * width] for k in range(3)]

    lat_shift = shift_ref[:1, :1]
    line = WLAT * levels
    cut = jnp.where(lax.axis_index("lat") == lat_count - 1, lat_shift * levels, line)

    def place_in_column(at, count):
        start = jnp.zeros_like(at)
        for c in range(1, count // line):
            start = jnp.where(at >= c * line, c * line, start)
        return at - start

    key_at = place_in_column(lax.broadcasted_iota(jnp.int32, (tokens, 1), 0), tokens)
    lane = lax.broadcasted_iota(jnp.int32, (1, GROUP * tokens), 1)
    query_at = place_in_column(lane, GROUP * tokens)
    key_side = jnp.where(key_at >= cut, 1.0, 0.0)
    query_side = jnp.where(query_at >= cut, 1.0, 0.0)
    allowed = key_side == query_side
    lane_head = lax.broadcasted_iota(jnp.int32, (tokens, lanes), 1) // head

    def stack(values):
        return jnp.concatenate(
            [jnp.where(lane_head == h, values, jnp.zeros_like(values)) for h in range(GROUP)],
            axis=0,
        )

    for group in range(HEADS // GROUP):
        low = group * lanes
        queries, keys_all, values_all = (part[:, low : low + lanes] for part in qkv)
        query_stack = stack(queries)
        grad_stack = stack(grad_heads[:, low : low + lanes])
        scores = dot(keys_all, query_stack, 1, 1) * inv_root
        weights_exp = jnp.where(allowed, jnp.exp(scores), 0.0)
        probability = weights_exp * (1.0 / jnp.sum(weights_exp, axis=0, keepdims=True))
        d_probability = dot(values_all, grad_stack, 1, 1)
        delta = jnp.sum(probability * d_probability, axis=0, keepdims=True)
        d_scores = (probability * (d_probability - delta)).astype(jnp.bfloat16)
        d_values = dot(probability.astype(jnp.bfloat16), grad_stack, 1, 0)
        d_keys = dot(d_scores, query_stack, 1, 0) * inv_root
        spread = dot(d_scores, keys_all, 0, 0)
        d_queries = jnp.zeros((tokens, lanes), jnp.float32)
        for h in range(GROUP):
            d_queries = jnp.where(lane_head == h, spread[h * tokens : (h + 1) * tokens], d_queries)
        d_queries = d_queries * inv_root
        joined_ref[:, low : low + lanes] = d_queries.astype(jnp.bfloat16)
        joined_ref[:, width + low : width + low + lanes] = d_keys.astype(jnp.bfloat16)
        joined_ref[:, 2 * width + low : 2 * width + low + lanes] = d_values.astype(jnp.bfloat16)
    d_normed = dot(joined_ref[...], w_qkv, 1, 1)
    branch = inv_std * (
        d_normed
        - jnp.mean(d_normed, axis=-1, keepdims=True)
        - normed * jnp.mean(d_normed * normed, axis=-1, keepdims=True)
    )
    out_ref[...] = (grads.astype(jnp.float32) + branch).astype(jnp.bfloat16)


def part_kernel(shift_ref, in_ref, kept_ref, moved_ref, before, after):
    tokens = in_ref.shape[0]
    levels, line = tokens // (WLAT * WLON), tokens // WLAT
    before[...] = in_ref[...].astype(jnp.float32)
    for r in range(WLAT):
        for c in range(WLON):
            low, to = levels * (c * WLAT + r), levels * (r * WLON + c)
            after[to : to + levels, :] = before[low : low + levels, :]
    at = lax.broadcasted_iota(jnp.int32, (tokens, 1), 0)
    moved = at < shift_ref[:1, :1] * line
    values = after[...]
    zero = jnp.zeros_like(values)
    kept_ref[...] = jnp.where(moved, zero, values)[line:].astype(jnp.bfloat16)
    moved_ref[...] = jnp.where(moved, values, zero)[: tokens - line].astype(jnp.bfloat16)


def join_kernel(kept_ref, moved_ref, out_hbm, sums, slabs, sems):
    levels = slabs.shape[1]
    tokens = sums.shape[0]
    line = tokens - kept_ref.shape[0]
    moved = moved_ref[...].astype(jnp.float32)
    kept = kept_ref[...].astype(jnp.float32)
    sums[:line, :] = moved[:line]
    sums[line : tokens - line, :] = kept[: tokens - 2 * line] + moved[line:]
    sums[tokens - line :, :] = kept[tokens - 2 * line :]
    copies = []
    count = slabs.shape[0] // 2
    for k in range(2):
        for i in range(k * count, (k + 1) * count):
            slabs[i] = sums[levels * i : levels * (i + 1), :].astype(jnp.bfloat16)
        half = pl.ds(k * count, count)
        copies.append(pltpu.make_async_copy(slabs.at[half], out_hbm.at[half], sems.at[k]))
        copies[-1].start()
    for copy in copies:
        copy.wait()


def local(block_inputs, out_grads, offsets, w_qkv, w_out):
    _, levels, rows, cols, width = block_inputs.shape
    tokens = levels * rows * cols
    flat = (rows * cols, levels, width)
    vmem = pl.BlockSpec(memory_space=pltpu.VMEM)
    smem = pl.BlockSpec(memory_space=pltpu.SMEM)
    both = (tokens, 2 * width)

    def held(*values):
        return [pltpu.with_memory_space_constraint(value, pltpu.VMEM) for value in values]

    hbm = pl.BlockSpec(memory_space=pl.ANY)
    lat_branch, lon_branch, lat_shift, block = pl.pallas_call(
        pack_kernel,
        out_shape=(
            pltpu.SMEM((1,), jnp.int32),
            pltpu.SMEM((1,), jnp.int32),
            pltpu.VMEM((8, 128), jnp.int32),
            pltpu.VMEM(both, jnp.bfloat16),
        ),
        in_specs=[hbm] * 3,
        out_specs=(smem, smem, vmem, vmem),
        scratch_shapes=[
            pltpu.SMEM(offsets.shape, jnp.int32),
            pltpu.VMEM(flat, jnp.bfloat16),
            pltpu.VMEM(flat, jnp.bfloat16),
            pltpu.VMEM(both, jnp.float32),
            pltpu.SemaphoreType.DMA((3,)),
        ],
        name="pack",
    )(
        offsets,
        block_inputs[0].transpose(1, 2, 0, 3).reshape(flat),
        out_grads[0].transpose(1, 2, 0, 3).reshape(flat),
    )
    lat_branch, lon_branch = lat_branch[0], lon_branch[0]
    (block,) = exchange_by(lat_branch, rows, block, "lat", False)
    block = pl.pallas_call(
        reorder_kernel,
        out_shape=pltpu.VMEM(both, jnp.bfloat16),
        in_specs=[vmem],
        out_specs=vmem,
        scratch_shapes=[pltpu.VMEM(both, jnp.float32)] * 2,
        name="reorder",
    )(*held(block))
    block, *weights = exchange_by(
        lon_branch, cols, block, "lon", False, (w_qkv[0], w_out[0])
    )
    result = pl.pallas_call(
        functools.partial(window_kernel, lat_count=lax.axis_size("lat")),
        out_shape=pltpu.VMEM((tokens, width), jnp.bfloat16),
        in_specs=[vmem] * 6,
        out_specs=vmem,
        scratch_shapes=[pltpu.VMEM((tokens, 3 * width), jnp.bfloat16)],
        name="window",
    )(*held(lat_shift, block, *weights))
    (result,) = exchange_by(lon_branch, cols, result, "lon", True)

    rest = pltpu.VMEM((tokens - tokens // rows, width), jnp.bfloat16)
    kept, moved = pl.pallas_call(
        part_kernel,
        out_shape=(rest, rest),
        in_specs=[vmem] * 2,
        out_specs=(vmem,) * 2,
        scratch_shapes=[pltpu.VMEM((tokens, width), jnp.float32)] * 2,
        name="part",
    )(*held(lat_shift, result))
    moved = shift(moved, section=-1, lat=1)
    kept = shift(kept, section=-1)
    joined = pl.pallas_call(
        join_kernel,
        out_shape=jax.ShapeDtypeStruct(flat, jnp.bfloat16),
        in_specs=[vmem] * 2,
        out_specs=hbm,
        scratch_shapes=[
            pltpu.VMEM((tokens, width), jnp.float32),
            pltpu.VMEM(flat, jnp.bfloat16),
            pltpu.SemaphoreType.DMA((2,)),
        ],
        name="join",
    )(*held(kept, moved))
    return joined.reshape(rows, cols, levels, width).transpose(2, 0, 1, 3)[None]


def solution(mesh):
    return jax.shard_map(
        local,
        mesh=mesh,
        in_specs=(
            P("section", None, "lat", "lon", None),
            P("section", None, "lat", "lon", None),
            P("section", None),
            P("section", None, None),
            P("section", None, None),
        ),
        out_specs=P("section", None, "lat", "lon", None),
        check_vma=False,
    )
```
